128 devices in a mesh: row: 8 (over z, y_lo), col: 16 (over y_hi, x, core).
Axes of the slice: x: 4, y: 4 (y_hi: 2, y_lo: 2; y = y_hi * 2 + y_lo), z: 4, core: 2. Of those that a mesh axis runs over, the one named last changes fastest.
Arguments:
- tiles: float32 [8, 16, 256, 128, 128], P('row', 'col'), may hold values from -0.125 to 0.125
- tile_rows: int32 [8, 16, 256], P('row', 'col'), may hold values from 0 to 255, as said below
- tile_cols: int32 [8, 16, 256], P('row', 'col'), may hold values from 0 to 127, as said below
- tile_counts: int32 [8, 16], P('row', 'col'), may hold values from 1 to 256, as said below
- block_now: float32 [8, 262144], P(None, ('row', 'col')), may hold values from -6 to 6
- block_prev: float32 [8, 262144], P(None, ('row', 'col')), may hold values from -6 to 6
- coupling: float32 [8, 8], replicated, may hold values from -3 to 3
- diag_energy: float32 [262144], P(('row', 'col')), may hold values from 1 to 4
Outputs:
- next_block: float32 [8, 262144], P(None, ('row', 'col'))
- alpha: float32 [8, 8], replicated
- beta: float32 [8, 8], replicated
The draws below stay inside these ranges and needn't reach their ends.
Inputs may be any that keep to these rules, and one draw needn't show every extreme that they name: `tile_rows`: every slot, used or not, holds a local tile row below 256; used tiles lie on or below the global diagonal. `tile_cols`: every slot holds a local tile column below 128. `tile_counts`: devices on the last block row use all 256 slots.
All inputs are finite; a program needn't handle non-finite values.
Results may differ from the reference program's by a relative error of at most 0.0003.
Values sent between devices are 32-bit elements; how exact they have to be, the bound alone decides.
A program may use at most 64 MiB of HBM per device.

```python
import jax
import jax.numpy as jnp
from jax import lax

VEC = 8
TILE = 128
CHT = 16
MAXT = 256
NDIM = 262144
N_ROW = 8
N_COL = 16


def tile_layout(key):
    base_key = jax.random.fold_in(key, 4242)
    keys = jax.random.split(base_key, 4)
    shape = (N_ROW, N_COL, MAXT)
    row_tiles = N_COL * CHT
    block_row = jnp.arange(N_ROW, dtype=jnp.int32)[:, None, None]
    block_col = jnp.arange(N_COL, dtype=jnp.int32)[None, :, None]
    source_row = jax.random.randint(keys[0], shape, 0, 1 << 20) % (block_row + 1)
    within = jax.random.randint(keys[1], shape, 0, CHT)
    raw_row = jax.random.randint(keys[2], shape, 0, row_tiles)
    lowest = block_col * CHT + within
    same_row = lowest + raw_row % (row_tiles - lowest)
    local_row = jnp.where(source_row == block_row, same_row, raw_row)
    local_col = source_row * CHT + within
    share = MAXT * (jnp.arange(N_ROW, dtype=jnp.int32) + 1) // N_ROW
    jitter = jax.random.randint(keys[3], (N_ROW, N_COL), 0, max(MAXT // (2 * N_ROW), 1) + 1)
    totals = jnp.maximum(share[:, None] - jitter, 1)
    totals = jnp.where(jnp.arange(N_ROW, dtype=jnp.int32)[:, None] == N_ROW - 1, MAXT, totals)
    return (local_row.astype(jnp.int32), local_col.astype(jnp.int32), totals.astype(jnp.int32))


def draw_tile_rows(key, part):
    return tile_layout(key)[0]


def draw_tile_cols(key, part):
    return tile_layout(key)[1]


def draw_tile_counts(key, part):
    return tile_layout(key)[2]


def level_of(key, dims, pieces, low, high):
    loudness = 1.0
    for position, blocks in pieces:
        draws = jax.random.uniform(jax.random.fold_in(jax.random.fold_in(key, 6), position), (blocks,), jnp.float32, low / len(pieces), high / len(pieces))
        loudness = loudness * jnp.repeat(jnp.exp(draws), dims[position] // blocks).reshape((-1,) + (1,) * (len(dims) - 1 - position))
    return loudness


def scatter_about(rng, shape, width, bound, shards=(), kind=jnp.bfloat16):
    array = jax.random.normal(rng, shape, jnp.float32) * width
    if len(shards) > 0:
        array = level_of(rng, shape, shards, -0.22, 0.18) * array
    return jnp.clip(array, min=-bound, max=bound).astype(kind)


def setup_inputs(seed: int = 0) -> dict:
    key_list = jax.random.split(jax.random.key(seed), 9)
    tiles = scatter_about(key_list[0], (N_ROW, N_COL, MAXT, TILE, TILE), (TILE * MAXT // CHT) ** -0.5, 0.125, ((0, 8), (1, 16)), jnp.float32)
    tile_rows = draw_tile_rows(jax.random.fold_in(key_list[8], 71), 0)
    tile_cols = draw_tile_cols(jax.random.fold_in(key_list[8], 71), 0)
    tile_counts = draw_tile_counts(jax.random.fold_in(key_list[8], 71), 0)
    block_now = scatter_about(key_list[4], (VEC, NDIM), 1.0, 6.0, ((1, 128),), jnp.float32)
    block_prev = scatter_about(key_list[5], (VEC, NDIM), 1.0, 6.0, ((1, 128),), jnp.float32)
    coupling = scatter_about(key_list[6], (VEC, VEC), 0.5, 3.0, (), jnp.float32)
    diag_energy = jnp.clip(1.0 + 3.0 * jax.random.uniform(key_list[7], (NDIM,), jnp.float32) ** level_of(key_list[7], (NDIM,), ((0, 128),), -0.2, 0.2), 1.0, 4.0)
    return dict(tiles=tiles, tile_rows=tile_rows, tile_cols=tile_cols, tile_counts=tile_counts, block_now=block_now, block_prev=block_prev, coupling=coupling, diag_energy=diag_energy)


def reference(tiles, tile_rows, tile_cols, tile_counts, block_now, block_prev, coupling, diag_energy):
    vectors = block_now.shape[0]
    tile_width = tiles.shape[-1]
    slot_count = tiles.shape[2]
    vector_tiles = block_now.reshape(vectors, -1, tile_width)
    grid_rows = jnp.arange(N_ROW, dtype=jnp.int32)[:, None] * jnp.ones((1, N_COL), jnp.int32)
    grid_cols = jnp.ones((N_ROW, 1), jnp.int32) * jnp.arange(N_COL, dtype=jnp.int32)[None, :]

    def visit(image, device_item):
        tile_block, rows_local, cols_local, tile_total, block_row, block_col = device_item
        global_row = (block_row * (N_COL * CHT) + rows_local).astype(jnp.int32)
        global_col = (cols_local // CHT * (N_COL * CHT) + block_col * CHT + cols_local % CHT).astype(jnp.int32)
        alive_mask = (jnp.arange(slot_count, dtype=jnp.int32) < tile_total).astype(vector_tiles.dtype)
        col_states = vector_tiles[:, global_col, :]
        row_states = vector_tiles[:, global_row, :]
        row_terms = jnp.einsum('vmk,mjk->vmj', col_states, tile_block, precision=lax.Precision.HIGHEST) * alive_mask[None, :, None]
        column_terms = jnp.einsum('vmj,mjk->vmk', row_states, tile_block, precision=lax.Precision.HIGHEST) * alive_mask[None, :, None]
        image = image.at[:, global_row, :].add(row_terms)
        image = image.at[:, global_col, :].add(column_terms)
        return (image, None)
    items = (tiles.reshape(-1, slot_count, tile_width, tile_width), tile_rows.reshape(-1, slot_count), tile_cols.reshape(-1, slot_count), tile_counts.reshape(-1), grid_rows.reshape(-1), grid_cols.reshape(-1))
    image, _ = lax.scan(visit, jnp.zeros_like(vector_tiles), items)
    image = image.reshape(vectors, -1) + diag_energy[None, :] * block_now
    alpha = jnp.dot(block_now, image.T, precision=lax.Precision.HIGHEST) / NDIM
    residual = image - jnp.dot(alpha.T, block_now, precision=lax.Precision.HIGHEST) - jnp.dot(coupling, block_prev, precision=lax.Precision.HIGHEST)
    gram_matrix = jnp.dot(residual, residual.T, precision=lax.Precision.HIGHEST) / NDIM
    factor = jnp.linalg.cholesky(gram_matrix)
    next_block = jax.scipy.linalg.solve_triangular(factor, residual, lower=True)
    return (next_block, alpha, factor.T)
```

```python
import functools

import jax
import jax.numpy as jnp
from jax import lax
from jax.experimental import pallas as pl
from jax.experimental.pallas import tpu as pltpu
from jax.sharding import PartitionSpec as P

MESH = pl.DeviceIdType.MESH
NT_DIMS = (((1,), (1,)), ((), ()))
NN_DIMS = (((1,), (0,)), ((), ()))
F32 = jnp.float32
BF16 = jnp.bfloat16
HIGHEST = lax.Precision.HIGHEST
CHUNK = 16


def dot_exact(left, right, dims):
    return lax.dot_general(left, right, dims, precision=HIGHEST, preferred_element_type=F32)


def split_rows(value):
    high = value.astype(BF16).astype(F32)
    return jnp.concatenate([high, value - high], axis=0).astype(BF16)


def kernel(
    total_states,
    tiles,
    rows_s,
    cols_s,
    count_s,
    rows_v,
    cols_v,
    now,
    prev,
    coupling,
    diag,
    next_out,
    alpha_out,
    beta_out,
    tile_f32,
    tile_hi,
    tile_lo,
    col_vec,
    row_vec,
    col_split,
    row_split,
    images,
    part_rows,
    part_cols,
    row_pair,
    row_ring,
    row_sum,
    row_last,
    col_ring,
    col_sum,
    col_last,
    image,
    resid,
    red_send,
    red_one,
    red_two,
    tile_sem,
    send_sem,
    col_sem,
    row_sem,
    pair_sem,
    ring_sem,
    last_sem,
    one_sem,
    two_sem,
):
    r = lax.axis_index("row")
    c = lax.axis_index("col")
    z, ylo = r // 2, r % 2
    yhi, x, core = c // 8, (c // 2) % 4, c % 2
    slots = tiles.shape[0]
    width = now.shape[1]

    def row_of(zz, yy):
        return zz * 2 + yy

    def col_of(yy, xx, cc):
        return yy * 8 + xx * 2 + cc

    zs = [(z + d) % 4 for d in range(1, 4)]
    xs = [(x + d) % 4 for d in range(1, 4)]
    row_peer = row_of(z, 1 - ylo)
    col_peer = col_of(1 - yhi, x, core)
    pair = col_of(yhi, x, 1 - core)

    chunks = slots // CHUNK

    def tile_copy(i):
        part = pl.ds(i * CHUNK, CHUNK)
        return pltpu.make_async_copy(tiles.at[part], tile_f32.at[part], tile_sem.at[i])

    for i in range(chunks):
        tile_copy(i).start()

    group_one = [(r, col_of(yhi, (x + d // 2) % 4, (core + d) % 2)) for d in range(1, 8)]
    group_two = [
        (row_of((z + d // 4) % 4, (ylo + d // 2) % 2), col_of((yhi + d) % 2, x, core))
        for d in range(1, 16)
    ]
    barrier = pltpu.get_barrier_semaphore()
    for peer in group_one + group_two:
        pl.semaphore_signal(barrier, inc=1, device_id=peer, device_id_type=MESH)

    def piece(ref, p):
        return ref.at[:, pl.ds(pl.multiple_of(p * width, width), width)]

    piece(col_vec, r)[...] = now[...]
    piece(row_vec, c)[...] = now[...]
    pl.semaphore_wait(barrier, len(group_one) + len(group_two))

    sends = []

    def send(src, dst, recv, peer):
        copy = pltpu.make_async_remote_copy(
            src_ref=src,
            dst_ref=dst,
            send_sem=send_sem.at[len(sends)],
            recv_sem=recv,
            device_id=peer,
            device_id_type=MESH,
        )
        copy.start()
        sends.append(copy)

    def arrived(dst, recv, peer):
        pltpu.make_async_remote_copy(
            src_ref=dst,
            dst_ref=dst,
            send_sem=send_sem.at[0],
            recv_sem=recv,
            device_id=peer,
            device_id_type=MESH,
        ).wait_recv()

    send(now, piece(col_vec, r), col_sem.at[r], (row_peer, c))
    send(now, piece(row_vec, c), row_sem.at[c], (r, col_peer))
    for zz in zs:
        send(now, piece(col_vec, r), col_sem.at[r], (row_of(zz, ylo), c))
    for xx in xs:
        send(now, piece(row_vec, c), row_sem.at[c], (r, col_of(yhi, xx, core)))
    send(now, piece(row_vec, c), row_sem.at[c], (r, pair))

    def convert(first, last):
        def chunk(i, _):
            tile_copy(i).wait()

            def one(j, _):
                value = tile_f32[i * CHUNK + j]
                high = value.astype(BF16)
                tile_hi[i * CHUNK + j] = high
                tile_lo[i * CHUNK + j] = (value - high.astype(F32)).astype(BF16)
                return 0

            lax.fori_loop(0, CHUNK, one, 0, unroll=4)
            return 0

        lax.fori_loop(first, last, chunk, 0)

    convert(0, 6)
    arrived(piece(col_vec, row_peer), col_sem.at[row_peer], (row_peer, c))
    for zz in zs:
        send(
            piece(col_vec, row_peer), piece(col_vec, row_peer), col_sem.at[row_peer], (row_of(zz, ylo), c)
        )
    arrived(piece(row_vec, col_peer), row_sem.at[col_peer], (r, col_peer))
    for xx in xs:
        send(
            piece(row_vec, col_peer),
            piece(row_vec, col_peer),
            row_sem.at[col_peer],
            (r, col_of(yhi, xx, core)),
        )
    send(piece(row_vec, col_peer), piece(row_vec, col_peer), row_sem.at[col_peer], (r, pair))
    convert(6, 10)

    def relay(yy):
        for xx in xs:
            p = col_of(yy, xx, core)
            arrived(piece(row_vec, p), row_sem.at[p], (r, col_of(yhi, xx, core)))
            send(piece(row_vec, p), piece(row_vec, p), row_sem.at[p], (r, pair))

    relay(yhi)
    convert(10, chunks)
    relay(1 - yhi)
    for yy in (ylo, 1 - ylo):
        for zz in zs:
            p = row_of(zz, yy)
            arrived(piece(col_vec, p), col_sem.at[p], (row_of(zz, ylo), c))

    def split_vectors(src, dst):
        def one(t, _):
            dst[t] = split_rows(src[:, pl.ds(pl.multiple_of(t * 128, 128), 128)])
            return 0

        lax.fori_loop(0, dst.shape[0], one, 0, unroll=8)

    split_vectors(col_vec, col_split)

    def products(first, last, index, vectors, transposed):
        unroll = 8

        def body(g, _):
            for u in range(unroll):
                m = g * unroll + u
                left = vectors[index[m]]
                if transposed:
                    weights = jnp.concatenate([tile_hi[m], tile_lo[m]], axis=0)
                    out = lax.dot_general(left, weights, NT_DIMS, preferred_element_type=F32)
                else:
                    weights = jnp.concatenate([tile_hi[m], tile_lo[m]], axis=1)
                    out = lax.dot_general(left, weights, NN_DIMS, preferred_element_type=F32)
                total = (out[0:8, 0:128] + out[8:16, 0:128]) + out[0:8, 128:256]
                images[pl.ds(m, 8, stride=slots), :] = total
            return 0

        lax.fori_loop(first // unroll, last // unroll, body, 0)

    used = lax.broadcasted_iota(jnp.int32, (1, slots), 1) < count_s[0, 0]

    def scatter(place, dst):
        count = dst.shape[1]
        wanted = jnp.where(used, place, -1)
        pick = (
            (lax.broadcasted_iota(jnp.int32, (count, slots), 0) == wanted).astype(F32).astype(BF16)
        )

        def one(v, _):
            value = images[pl.ds(pl.multiple_of(v * slots, slots), slots), :]
            high = value.astype(BF16)
            low = (value - high.astype(F32)).astype(BF16)
            out = lax.dot_general(
                pick, jnp.concatenate([high, low], axis=1), NN_DIMS, preferred_element_type=F32
            )
            dst[v] = out[:, 0:128] + out[:, 128:256]
            return 0

        lax.fori_loop(0, 8, one, 0)

    products(0, slots, cols_s, col_split, True)
    place = rows_v[...]
    owner = place // 16
    place = ((owner % 2) * 8 + ((owner // 2) % 4) * 2 + owner // 8) * 16 + place % 16
    scatter(place, part_rows)
    half = part_rows.shape[1] // 2

    def half_of(cc):
        return part_rows.at[:, pl.ds(pl.multiple_of(cc * half, half), half), :]

    send(half_of(1 - core), row_pair, pair_sem.at[0], (r, pair))

    for yy in (yhi, 1 - yhi):
        for xx in [x] + xs:
            if yy is yhi and xx is x:
                p = col_of(yhi, x, 1 - core)
            else:
                p = col_of(yy, xx, 1 - core)
            arrived(piece(row_vec, p), row_sem.at[p], (r, pair))
    split_vectors(row_vec, row_split)
    mid = slots // 4
    products(0, mid, rows_s, row_split, False)

    arrived(row_pair, pair_sem.at[0], (r, pair))
    mine = half_of(core)

    def add_pair(v, _):
        row_pair[v] = row_pair[v] + mine[v]
        return 0

    lax.fori_loop(0, 8, add_pair, 0)
    for d, xx in enumerate(xs):
        send(
            row_pair.at[:, pl.ds(pl.multiple_of(xx * 32, 32), 32), :],
            row_ring.at[d],
            ring_sem.at[d],
            (r, col_of(yhi, xx, core)),
        )
    products(mid, slots, rows_s, row_split, False)
    scatter(cols_v[...], part_cols)
    for d, zz in enumerate(zs):
        send(
            part_cols.at[:, pl.ds(pl.multiple_of(zz * 32, 32), 32), :],
            col_ring.at[d],
            ring_sem.at[3 + d],
            (row_of(zz, ylo), c),
        )

    flat_rows = part_rows.reshape(8 * part_rows.shape[1], 128)
    stride = part_rows.shape[1]

    def inner(q, acc):
        owner = (q % 2) * 8 + ((q // 2) % 4) * 2 + q // 8
        left = jnp.concatenate([row_split[owner * 16 + t] for t in range(16)], axis=1)
        right = jnp.concatenate(
            [split_rows(flat_rows[pl.ds(q * 16 + t, 8, stride=stride), :]) for t in range(16)], axis=1
        )
        return acc + lax.dot_general(left, right, NT_DIMS, preferred_element_type=F32)

    both = lax.fori_loop(0, 16, inner, jnp.zeros((16, 16), F32))
    cross = (both[0:8, 0:8] + both[8:16, 0:8]) + both[0:8, 8:16]
    eye = (
        lax.broadcasted_iota(jnp.int32, (8, 8), 0) == lax.broadcasted_iota(jnp.int32, (8, 8), 1)
    ).astype(F32)

    def diag_of(t):
        return diag[t : t + 1, :]

    def now_of(t):
        return now[:, t * 128 : (t + 1) * 128]

    count = width // 128
    weighted = jnp.concatenate([now_of(t) * diag_of(t) for t in range(count)], axis=1)
    cross = cross + dot_exact(eye, cross, NT_DIMS) + dot_exact(now[...], weighted, NT_DIMS)

    def reduce_send(k, value):
        red_send[k, :, 0:8] = value
        slot = x * 2 + core
        red_one[k, slot, :, 0:8] = value
        for peer in group_one:
            send(red_send.at[k], red_one.at[k, slot], one_sem.at[k, slot], peer)

    def reduce_pass(k):
        for d in range(1, 8):
            slot = ((x + d // 2) % 4) * 2 + (core + d) % 2
            arrived(red_one.at[k, slot], one_sem.at[k, slot], group_one[d - 1])
        total = red_one[k, 0, :, 0:8]
        for i in range(1, 8):
            total = total + red_one[k, i, :, 0:8]
        red_send[2 + k, :, 0:8] = total
        slot = r * 2 + yhi
        red_two[k, slot, :, 0:8] = total
        for peer in group_two:
            send(red_send.at[2 + k], red_two.at[k, slot], two_sem.at[k, slot], peer)

    def reduce_end(k):
        for d in range(1, 16):
            slot = row_of((z + d // 4) % 4, (ylo + d // 2) % 2) * 2 + (yhi + d) % 2
            arrived(red_two.at[k, slot], two_sem.at[k, slot], group_two[d - 1])
        total = red_two[k, 0, :, 0:8]
        for i in range(1, 16):
            total = total + red_two[k, i, :, 0:8]
        return total

    red_send[...] = jnp.zeros_like(red_send)
    reduce_send(0, cross)

    def ring_total(own, own_at, ring, base, dst, peers):
        for d in range(3):
            arrived(ring.at[d], ring_sem.at[base + d], peers[d])

        def one(v, _):
            own_part = own[v, pl.ds(pl.multiple_of(own_at * 32, 32), 32), :]
            dst[v] = (own_part + ring[0, v]) + (ring[1, v] + ring[2, v])
            return 0

        lax.fori_loop(0, 8, one, 0)

    def lot(ref, k):
        return ref.at[:, pl.ds(pl.multiple_of(k * 16, 16), 16), :]

    row_from = [(r, col_of(yhi, (x + 3 - d) % 4, core)) for d in range(3)]
    col_from = [(row_of((z + 3 - d) % 4, ylo), c) for d in range(3)]
    ring_total(row_pair, x, row_ring, 0, row_sum, row_from)
    send(lot(row_sum, 1 - yhi), row_last, last_sem.at[0], (r, col_peer))
    reduce_pass(0)
    ring_total(part_cols, z, col_ring, 3, col_sum, col_from)
    send(lot(col_sum, 1 - ylo), col_last, last_sem.at[1], (row_peer, c))
    scale = 1.0 / total_states
    alpha = reduce_end(0) * scale
    alpha_out[...] = alpha
    alpha_t = dot_exact(eye, alpha, NT_DIMS)
    taken = dot_exact(alpha_t, now[...], NN_DIMS) + dot_exact(coupling[...], prev[...], NN_DIMS)

    arrived(row_last, last_sem.at[0], (r, col_peer))
    arrived(col_last, last_sem.at[1], (row_peer, c))
    row_mine, col_mine = lot(row_sum, yhi), lot(col_sum, ylo)
    for v in range(8):
        image[v * 16 : (v + 1) * 16, :] = (row_mine[v] + row_last[v]) + (col_mine[v] + col_last[v])
    for t in range(count):
        value = image[pl.ds(t, 8, stride=16), :] + diag_of(t) * now_of(t)
        resid[:, t * 128 : (t + 1) * 128] = value - taken[:, t * 128 : (t + 1) * 128]
    residual = resid[...]
    reduce_send(1, dot_exact(residual, residual, NT_DIMS))
    reduce_pass(1)
    gram = reduce_end(1) * scale

    work = jnp.concatenate([gram, eye], axis=1)
    line = lax.broadcasted_iota(jnp.int32, (8, 16), 0)
    for j in range(8):
        lead = jnp.broadcast_to(work[j : j + 1, :], (8, 16))
        column = jnp.broadcast_to(work[:, j : j + 1], (8, 16))
        pivot = jnp.broadcast_to(work[j : j + 1, j : j + 1], (8, 16))
        root = jnp.sqrt(pivot)
        scaled = lead / root
        work = jnp.where(
            line == j, scaled, jnp.where(line > j, work - (column / root) * scaled, work)
        )
    upper = lax.broadcasted_iota(jnp.int32, (8, 8), 0) <= lax.broadcasted_iota(jnp.int32, (8, 8), 1)
    beta_out[...] = jnp.where(upper, work[:, 0:8], 0.0)
    next_out[...] = dot_exact(work[:, 8:16], residual, NN_DIMS)

    for copy in sends:
        copy.wait_send()


def local(tiles, tile_rows, tile_cols, tile_counts, block_now, block_prev, coupling, diag_energy):
    slots, tile_width = tiles.shape[2], tiles.shape[3]
    vectors, width = block_now.shape
    n_row, n_col = lax.axis_size("row"), lax.axis_size("col")
    count = width // tile_width
    rows, cols = tile_rows.reshape(1, slots), tile_cols.reshape(1, slots)
    vmem = pl.BlockSpec(memory_space=pltpu.VMEM)
    smem = pl.BlockSpec(memory_space=pltpu.SMEM)
    dma = pltpu.SemaphoreType.DMA
    n_rt, n_ct = n_col * count, n_row * count
    shape = jax.ShapeDtypeStruct
    return pl.pallas_call(
        functools.partial(kernel, width * n_row * n_col),
        out_shape=(shape((vectors, width), F32), shape((8, 8), F32), shape((8, 8), F32)),
        in_specs=[pl.BlockSpec(memory_space=pl.ANY), smem, smem, smem, vmem, vmem, vmem, vmem, vmem, vmem],
        out_specs=(vmem, vmem, vmem),
        scratch_shapes=[
            pltpu.VMEM((slots, tile_width, tile_width), F32),
            pltpu.VMEM((slots, tile_width, tile_width), BF16),
            pltpu.VMEM((slots, tile_width, tile_width), BF16),
            pltpu.VMEM((vectors, n_row * width), F32),
            pltpu.VMEM((vectors, n_col * width), F32),
            pltpu.VMEM((n_ct, 16, tile_width), BF16),
            pltpu.VMEM((n_rt, 16, tile_width), BF16),
            pltpu.VMEM((vectors * slots, tile_width), F32),
            pltpu.VMEM((vectors, n_rt, tile_width), F32),
            pltpu.VMEM((vectors, n_ct, tile_width), F32),
            pltpu.VMEM((vectors, n_rt // 2, tile_width), F32),
            pltpu.VMEM((3, vectors, 2 * count, tile_width), F32),
            pltpu.VMEM((vectors, 2 * count, tile_width), F32),
            pltpu.VMEM((vectors, count, tile_width), F32),
            pltpu.VMEM((3, vectors, 2 * count, tile_width), F32),
            pltpu.VMEM((vectors, 2 * count, tile_width), F32),
            pltpu.VMEM((vectors, count, tile_width), F32),
            pltpu.VMEM((vectors * count, tile_width), F32),
            pltpu.VMEM((vectors, width), F32),
            pltpu.VMEM((4, 8, 128), F32),
            pltpu.VMEM((2, 8, 8, 128), F32),
            pltpu.VMEM((2, 16, 8, 128), F32),
            dma((slots // CHUNK,)),
            dma((80,)),
            dma((n_row,)),
            dma((n_col,)),
            dma((1,)),
            dma((6,)),
            dma((2,)),
            dma((2, 8)),
            dma((2, 16)),
        ],
        compiler_params=pltpu.CompilerParams(
            collective_id=0, has_side_effects=True, vmem_limit_bytes=60 * 2**20
        ),
    )(
        tiles.reshape(slots, tile_width, tile_width),
        rows.reshape(slots),
        cols.reshape(slots),
        tile_counts,
        rows,
        cols,
        block_now,
        block_prev,
        coupling,
        diag_energy.reshape(count, tile_width),
    )


def solution(mesh):
    return jax.shard_map(
        local,
        mesh=mesh,
        in_specs=(
            P("row", "col", None, None, None),
            P("row", "col", None),
            P("row", "col", None),
            P("row", "col"),
            P(None, ("row", "col")),
            P(None, ("row", "col")),
            P(),
            P(("row", "col")),
        ),
        out_specs=(P(None, ("row", "col")), P(), P()),
        check_vma=False,
    )
```

```python
import functools
import itertools

import jax
import jax.numpy as jnp
from jax import lax
from jax.experimental import pallas as pl
from jax.experimental.pallas import tpu as pltpu
from jax.sharding import PartitionSpec as P

MESH = pl.DeviceIdType.MESH
NT_DIMS = (((1,), (1,)), ((), ()))
NN_DIMS = (((1,), (0,)), ((), ()))
F32 = jnp.float32
BF16 = jnp.bfloat16
HIGHEST = lax.Precision.HIGHEST
CHUNK = 16
UNROLL = 64
SHIFT = 2.5


def dot_exact(left, right, dims):
    return lax.dot_general(left, right, dims, precision=HIGHEST, preferred_element_type=F32)


def split_rows(value):
    high = value.astype(BF16).astype(F32)
    return jnp.concatenate([high, value - high], axis=0).astype(BF16)


def iota(shape, axis):
    return lax.broadcasted_iota(jnp.int32, shape, axis)


def kernel(
    tiles,
    rows_h,
    cols_h,
    count_h,
    rows_w,
    cols_w,
    now_h,
    prev_h,
    diag_h,
    shifted_out,
    early_out,
    final_out,
    tile_f32,
    tile_hi,
    tile_lo,
    rows_s,
    cols_s,
    count_s,
    rows_v,
    cols_v,
    lanczos,
    diag,
    col_vec,
    row_vec,
    col_split,
    row_split,
    images,
    part_rows,
    part_cols,
    row_pair,
    row_ring,
    row_sum,
    row_last,
    col_near,
    col_far,
    col_send,
    col_last,
    image,
    shifted,
    early_send,
    early_one,
    early_two,
    final_send,
    final_all,
    final_sum,
    tile_sem,
    in_sem,
    send_sem,
    col_sem,
    row_sem,
    pair_sem,
    ring_sem,
    last_sem,
    back_sem,
    one_sem,
    two_sem,
    all_sem,
):
    r = lax.axis_index("row")
    c = lax.axis_index("col")
    z, ylo = r // 2, r % 2
    yhi, x, core = c // 8, (c // 2) % 4, c % 2
    slots = tiles.shape[0]
    width = now_h.shape[1]
    count = width // 128
    open_scope = []

    def phase(name):
        if open_scope:
            open_scope.pop().__exit__(None, None, None)
        if name:
            open_scope.append(jax.named_scope(name))
            open_scope[0].__enter__()

    def row_of(zz, yy):
        return zz * 2 + yy

    def col_of(yy, xx, cc):
        return yy * 8 + xx * 2 + cc

    zs = [(z + d) % 4 for d in (2, 1, 3)]
    xs = [(x + d) % 4 for d in (2, 1, 3)]
    row_peer = row_of(z, 1 - ylo)
    col_peer = col_of(1 - yhi, x, core)
    pair = col_of(yhi, x, 1 - core)
    zn = zs[1:]
    far = (row_of(zs[0], 1 - ylo), c)
    col_steps = [(2, 1), (1, 1), (3, 1), (2, 0), (0, 1), (1, 0), (3, 0)]
    col_group = [(row_of((z + a) % 4, (ylo + b) % 2), c) for a, b in col_steps]
    col_back = [(row_of((z + 4 - a) % 4, (ylo + b) % 2), c) for a, b in col_steps]

    phase("start")
    barrier = pltpu.get_barrier_semaphore()
    first_peers = [(row_peer, c), (r, col_peer), far] + [(row_of(zz, ylo), c) for zz in zs]
    first_peers += [(r, col_of(yhi, xx, core)) for xx in xs] + [(r, pair)]
    for peer in first_peers:
        pl.semaphore_signal(barrier, inc=1, device_id=peer, device_id_type=MESH)

    now, prev = lanczos.at[0:8], lanczos.at[8:16]
    loads = [
        pltpu.make_async_copy(src, dst, in_sem.at[i])
        for i, (src, dst) in enumerate(
            [
                (now_h, now),
                (prev_h, prev),
                (diag_h, diag),
                (rows_h, rows_s),
                (cols_h, cols_s),
                (count_h, count_s),
                (rows_w, rows_v),
                (cols_w, cols_v),
            ]
        )
    ]
    loads[0].start()
    chunks = slots // CHUNK

    def tile_copy(i):
        part = pl.ds(i * CHUNK, CHUNK)
        return pltpu.make_async_copy(tiles.at[part], tile_f32.at[part], tile_sem.at[i])

    def piece(ref, p):
        return ref.at[:, pl.ds(pl.multiple_of(p * width, width), width)]

    loads[0].wait()
    for i in range(chunks):
        tile_copy(i).start()
    for copy in loads[1:]:
        copy.start()
    phase("barrier")
    pl.semaphore_wait(barrier, len(first_peers))

    sends = []

    def send(src, dst, recv, peer):
        copy = pltpu.make_async_remote_copy(
            src_ref=src,
            dst_ref=dst,
            send_sem=send_sem.at[len(sends)],
            recv_sem=recv,
            device_id=peer,
            device_id_type=MESH,
        )
        copy.start()
        sends.append(copy)

    def arrived(dst, recv, peer):
        pltpu.make_async_remote_copy(
            src_ref=dst,
            dst_ref=dst,
            send_sem=send_sem.at[0],
            recv_sem=recv,
            device_id=peer,
            device_id_type=MESH,
        ).wait_recv()

    phase("send1")
    send(now, piece(col_vec, r), col_sem.at[r], (row_peer, c))
    send(now, piece(row_vec, c), row_sem.at[c], (r, col_peer))
    send(now, piece(col_vec, r), col_sem.at[r], far)
    for zz in zs:
        send(now, piece(col_vec, r), col_sem.at[r], (row_of(zz, ylo), c))
    for xx in xs:
        send(now, piece(row_vec, c), row_sem.at[c], (r, col_of(yhi, xx, core)))
    send(now, piece(row_vec, c), row_sem.at[c], (r, pair))
    piece(col_vec, r)[...] = now[...]
    piece(row_vec, c)[...] = now[...]

    def convert(first, last):
        def chunk(i, _):
            tile_copy(i).wait()

            def one(j, _):
                value = tile_f32[i * CHUNK + j]
                high = value.astype(BF16)
                tile_hi[i * CHUNK + j] = high
                tile_lo[i * CHUNK + j] = (value - high.astype(F32)).astype(BF16)
                return 0

            lax.fori_loop(0, CHUNK, one, 0, unroll=8)
            return 0

        lax.fori_loop(first, last, chunk, 0)

    phase("conv1")
    convert(0, 9)
    phase("fwdrow")
    arrived(piece(col_vec, row_peer), col_sem.at[row_peer], (row_peer, c))
    for zz in zn:
        send(
            piece(col_vec, row_peer), piece(col_vec, row_peer), col_sem.at[row_peer], (row_of(zz, ylo), c)
        )
    phase("fwdcol")
    arrived(piece(row_vec, col_peer), row_sem.at[col_peer], (r, col_peer))
    for xx in xs:
        send(
            piece(row_vec, col_peer),
            piece(row_vec, col_peer),
            row_sem.at[col_peer],
            (r, col_of(yhi, xx, core)),
        )
    send(piece(row_vec, col_peer), piece(row_vec, col_peer), row_sem.at[col_peer], (r, pair))
    phase("conv2")
    convert(9, chunks)
    for copy in loads[1:]:
        copy.wait()
    phase("early")
    early_send[...] = jnp.zeros_like(early_send)
    known = lanczos[...]
    early_send[0, :, 0:16] = dot_exact(known, known, NT_DIMS)

    phase("waitcolvec")
    for zz in zn:
        for yy in (ylo, 1 - ylo):
            p = row_of(zz, yy)
            arrived(piece(col_vec, p), col_sem.at[p], (row_of(zz, ylo), c))
    for p in (row_of(zs[0], ylo), far[0]):
        arrived(piece(col_vec, p), col_sem.at[p], (p, c))

    def split_vectors(src, dst):
        def one(t, _):
            dst[t] = split_rows(src[:, pl.ds(pl.multiple_of(t * 128, 128), 128)])
            return 0

        lax.fori_loop(0, dst.shape[0], one, 0, unroll=16)

    phase("split1")
    split_vectors(col_vec, col_split)

    def products(first, last, index, vectors, transposed):
        def body(g, _):
            for u in range(UNROLL):
                m = g * UNROLL + u
                left = vectors[index[m]]
                if transposed:
                    weights = jnp.concatenate([tile_hi[m], tile_lo[m]], axis=0)
                    out = lax.dot_general(left, weights, NT_DIMS, preferred_element_type=F32)
                else:
                    weights = jnp.concatenate([tile_hi[m], tile_lo[m]], axis=1)
                    out = lax.dot_general(left, weights, NN_DIMS, preferred_element_type=F32)
                total = (out[0:8, 0:128] + out[8:16, 0:128]) + out[0:8, 128:256]
                images[pl.ds(m, 8, stride=slots), :] = total
            return 0

        lax.fori_loop(first // UNROLL, last // UNROLL, body, 0)

    used = iota((1, slots), 1) < count_s[0, 0]

    def scatter(place, dst):
        wanted = jnp.where(used, place, -1)
        pick = (iota((dst.shape[1], slots), 0) == wanted).astype(F32).astype(BF16)
        for v in range(8):
            value = images[v * slots : (v + 1) * slots, :]
            high = value.astype(BF16)
            low = (value - high.astype(F32)).astype(BF16)
            out = lax.dot_general(
                pick, jnp.concatenate([high, low], axis=1), NN_DIMS, preferred_element_type=F32
            )
            dst[v] = out[:, 0:128] + out[:, 128:256]

    phase("prodrows1")
    products(0, 2 * UNROLL, cols_s, col_split, True)
    phase("relay")
    for yy in (yhi, 1 - yhi):
        for xx in xs:
            p = col_of(yy, xx, core)
            arrived(piece(row_vec, p), row_sem.at[p], (r, col_of(yhi, xx, core)))
            send(piece(row_vec, p), piece(row_vec, p), row_sem.at[p], (r, pair))
    phase("prodrows2")
    products(2 * UNROLL, slots, cols_s, col_split, True)
    phase("scatrows")
    place = rows_v[...]
    owner = place // 16
    scatter(
        ((owner % 2) * 8 + ((owner // 2) % 4) * 2 + owner // 8) * 16 + place % 16, part_rows
    )
    half = part_rows.shape[1] // 2

    def half_of(cc):
        return part_rows.at[:, pl.ds(pl.multiple_of(cc * half, half), half), :]

    send(half_of(1 - core), row_pair, pair_sem.at[0], (r, pair))

    phase("waitrowvec")
    for yy in (yhi, 1 - yhi):
        for xx in [x] + xs:
            p = col_of(yy, xx, 1 - core)
            arrived(piece(row_vec, p), row_sem.at[p], (r, pair))
    row_steps = list(itertools.product(range(2), range(4), range(2)))[1:]
    row_group = [(r, col_of((yhi + a) % 2, (x + b) % 4, (core + d) % 2)) for a, b, d in row_steps]
    row_back = [
        (r, col_of((yhi + a) % 2, (x + 4 - b) % 4, (core + d) % 2)) for a, b, d in row_steps
    ]
    phase("split2")
    split_vectors(row_vec, row_split)
    phase("prodcols1")
    products(0, UNROLL, rows_s, row_split, False)
    phase("waitpair")
    arrived(row_pair, pair_sem.at[0], (r, pair))
    mine = half_of(core)
    for v in range(8):
        row_pair[v] = row_pair[v] + mine[v]
    for d, xx in enumerate(xs):
        send(
            row_pair.at[:, pl.ds(pl.multiple_of(xx * 2 * count, 2 * count), 2 * count), :],
            row_ring.at[d],
            ring_sem.at[d],
            (r, col_of(yhi, xx, core)),
        )
    early_one[c] = early_send[0]
    for peer in row_group:
        send(early_send.at[0], early_one.at[c], one_sem.at[c], peer)
    phase("prodcols2")
    products(UNROLL, slots, rows_s, row_split, False)
    phase("scatcols")
    scatter(cols_v[...], part_cols)

    def lot(ref, k):
        return ref.at[:, pl.ds(pl.multiple_of(k * count, count), count), :]

    for d, zz in enumerate(zn):
        send(
            part_cols.at[:, pl.ds(pl.multiple_of(zz * 2 * count, 2 * count), 2 * count), :],
            col_near.at[d],
            back_sem.at[d],
            (row_of(zz, ylo), c),
        )
    send(lot(part_cols, far[0]), col_far.at[0], back_sem.at[2], far)
    send(
        lot(part_cols, row_of(zs[0], ylo)), col_far.at[1], back_sem.at[3], (row_of(zs[0], ylo), c)
    )

    phase("near")
    for d in range(2):
        arrived(col_near.at[d], back_sem.at[d], (row_of(zn[1 - d], ylo), c))
    at = pl.multiple_of((1 - ylo) * count, count)
    away = lot(part_cols, row_peer)
    for v in range(8):
        col_send[v] = away[v] + (col_near[0, v, pl.ds(at, count), :] + col_near[1, v, pl.ds(at, count), :])
    send(col_send, col_last, last_sem.at[1], (row_peer, c))

    phase("ringrow")
    for d in range(3):
        back = (x + (2, 3, 1)[d]) % 4
        arrived(row_ring.at[d], ring_sem.at[d], (r, col_of(yhi, back, core)))
    for v in range(8):
        own = row_pair[v, pl.ds(pl.multiple_of(x * 2 * count, 2 * count), 2 * count), :]
        row_sum[v] = (own + row_ring[0, v]) + (row_ring[1, v] + row_ring[2, v])
    send(lot(row_sum, 1 - yhi), row_last, last_sem.at[0], (r, col_peer))

    phase("waitfar")
    arrived(col_far.at[0], back_sem.at[2], far)
    arrived(col_far.at[1], back_sem.at[3], (row_of(zs[0], ylo), c))
    home = pl.multiple_of(ylo * count, count)
    row_mine, col_mine = lot(row_sum, yhi), lot(part_cols, r)
    for v in range(8):
        near = col_near[0, v, pl.ds(home, count), :] + col_near[1, v, pl.ds(home, count), :]
        total = (row_mine[v] + col_mine[v]) + (col_far[0, v] + col_far[1, v])
        image[v * count : (v + 1) * count, :] = total + near
    phase("early1")
    for peer in row_back:
        arrived(early_one.at[peer[1]], one_sem.at[peer[1]], peer)
    total = early_one[0]
    for i in range(1, early_one.shape[0]):
        total = total + early_one[i]
    early_send[1] = total
    early_two[r] = total
    for peer in col_group:
        send(early_send.at[1], early_two.at[r], two_sem.at[r], peer)
    phase("waitlast")
    arrived(col_last, last_sem.at[1], (row_peer, c))
    arrived(row_last, last_sem.at[0], (r, col_peer))
    phase("shifted")
    for v in range(8):
        part = slice(v * count, (v + 1) * count)
        image[part, :] = image[part, :] + (row_last[v] + col_last[v])
    for t in range(count):
        at = slice(t * 128, (t + 1) * 128)
        shifted[:, at] = image[pl.ds(t, 8, stride=count), :] + (diag[t : t + 1, :] - SHIFT) * now[:, at]
    shifted_copy = pltpu.make_async_copy(shifted, shifted_out, in_sem.at[0])
    shifted_copy.start()

    phase("gram")
    value = shifted[...]
    gram = dot_exact(value, jnp.concatenate([value, lanczos[...]], axis=0), NT_DIMS)
    place, lane = iota((24, 256), 0), iota((24, 256), 1)
    spread = ((lane // 64 == place // 8) & (lane % 8 == place % 8)).astype(F32)
    flat = dot_exact(gram, spread, NN_DIMS)
    flat = jnp.where((iota((8, 256), 1) // 8) % 8 == iota((8, 256), 0), flat, 0.0)
    flat = jnp.sum(flat, axis=0, keepdims=True)
    final_send[0:1, :] = flat[:, 0:128]
    final_send[1:2, :] = flat[:, 128:256]
    phase("final")
    me = r * early_one.shape[0] + c
    own_copy = pltpu.make_async_copy(final_send, final_all.at[me], in_sem.at[2])
    own_copy.start()
    steps = sorted(
        itertools.product(range(4), range(2), range(2), range(4), range(2)),
        key=lambda s: -(min(s[0], 4 - s[0]) + s[1] + 2 * s[2] + min(s[3], 4 - s[3])),
    )
    steps.remove((0, 0, 0, 0, 0))
    lasts = []
    for a, b, d, e, f in steps:
        peer = (
            row_of((z + a) % 4, (ylo + b) % 2),
            col_of((yhi + d) % 2, (x + e) % 4, (core + f) % 2),
        )
        copy = pltpu.make_async_remote_copy(
            src_ref=final_send,
            dst_ref=final_all.at[me],
            send_sem=all_sem.at[0],
            recv_sem=all_sem.at[1],
            device_id=peer,
            device_id_type=MESH,
        )
        copy.start()
        lasts.append(peer)
    phase("early2")
    for peer in col_back:
        arrived(early_two.at[peer[0]], two_sem.at[peer[0]], peer)
    total = early_two[0]
    for i in range(1, early_two.shape[0]):
        total = total + early_two[i]
    early_send[2] = total
    early_copy = pltpu.make_async_copy(early_send.at[2], early_out, in_sem.at[1])
    early_copy.start()

    phase("waitfinal")
    own_copy.wait()
    others = final_all.at[0 : len(steps)]
    waiter = pltpu.make_async_remote_copy(
        src_ref=others,
        dst_ref=others,
        send_sem=all_sem.at[0],
        recv_sem=all_sem.at[1],
        device_id=lasts[0],
        device_id_type=MESH,
    )
    waiter.wait_recv()
    phase("sum")
    final_sum[...] = jnp.sum(final_all[...], axis=0)
    final_copy = pltpu.make_async_copy(final_sum, final_out, in_sem.at[2])
    final_copy.start()
    phase("waitsends")
    for copy in sends:
        copy.wait_send()
    waiter.wait_send()
    shifted_copy.wait()
    early_copy.wait()
    final_copy.wait()
    phase(None)


def finish(scale, shifted, early, final, now, prev, coupling, next_out, alpha_out, beta_out):
    line, lane = iota((8, 16), 0), iota((8, 16), 1)
    flat = jnp.concatenate([final[0:1, :], final[1:2, :]], axis=1) * scale
    flat = jnp.where((iota((8, 256), 1) // 8) % 8 == iota((8, 256), 0), flat, 0.0)
    high = flat.astype(BF16)
    rest = flat - high.astype(F32)
    mid = rest.astype(BF16)
    low = (rest - mid.astype(F32)).astype(BF16)
    parts = jnp.concatenate([high.astype(F32), mid.astype(F32), low.astype(F32)], axis=0).astype(BF16)
    place, at = iota((16, 256), 0), iota((16, 256), 1)

    def gathered(block):
        pick = ((at // 64 == block) & (at % 8 == place % 8)).astype(F32).astype(BF16)
        out = lax.dot_general(parts, pick, NT_DIMS, preferred_element_type=F32)
        return (out[0:8] + out[8:16]) + out[16:24]

    cross = gathered(1 + place // 8)
    square = gathered(jnp.where(place < 8, 0, -1))
    known = early[:, 0:16] * scale
    eye = (line == lane).astype(F32)
    shift_eye = (line + 8 == lane).astype(F32)
    coupled = dot_exact(coupling[...], shift_eye, NN_DIMS)
    alpha_t = cross + SHIFT * known[0:8]
    weights = jnp.where(lane < 8, SHIFT * eye - alpha_t, -coupled)
    zeros = jnp.zeros((8, 16), F32)
    mixed = cross + 0.5 * dot_exact(weights, known, NN_DIMS)
    once = dot_exact(mixed, jnp.concatenate([weights, zeros], axis=0), NT_DIMS)
    again = dot_exact(weights, jnp.concatenate([mixed, zeros], axis=0), NT_DIMS)
    residual = shifted[...] + dot_exact(
        weights, jnp.concatenate([now[...], prev[...]], axis=0), NN_DIMS
    )
    work = (square + (once + again)) + shift_eye
    for j in range(8):
        lead = jnp.broadcast_to(work[j : j + 1, :], (8, 16))
        column = jnp.broadcast_to(work[:, j : j + 1], (8, 16))
        pivot = jnp.broadcast_to(work[j : j + 1, j : j + 1], (8, 16))
        work = jnp.where(line > j, work - (column / pivot) * lead, work)
    pivots = jnp.sum(jnp.where(line == lane, work, 0.0), axis=1, keepdims=True)
    work = work / jnp.sqrt(pivots)
    next_out[...] = dot_exact(work[:, 8:16], residual, NN_DIMS)
    beta_out[...] = jnp.where(line <= lane, work, 0.0)[:, 0:8]
    alpha_out[...] = dot_exact(eye[:, 0:8], alpha_t[:, 0:8], NT_DIMS)


def local(tiles, tile_rows, tile_cols, tile_counts, block_now, block_prev, coupling, diag_energy):
    slots, tile_width = tiles.shape[2], tiles.shape[3]
    vectors, width = block_now.shape
    n_row, n_col = lax.axis_size("row"), lax.axis_size("col")
    count = width // tile_width
    rows, cols = tile_rows.reshape(1, slots), tile_cols.reshape(1, slots)
    hbm = pl.BlockSpec(memory_space=pltpu.HBM)
    vmem = pl.BlockSpec(memory_space=pltpu.VMEM)
    dma = pltpu.SemaphoreType.DMA
    n_rt, n_ct = n_col * count, n_row * count
    shape = jax.ShapeDtypeStruct
    shifted, early, final = pl.pallas_call(
        kernel,
        out_shape=(shape((vectors, width), F32), shape((16, 128), F32), shape((2, 128), F32)),
        in_specs=[hbm] * 9,
        out_specs=(hbm, hbm, hbm),
        scratch_shapes=[
            pltpu.VMEM((slots, tile_width, tile_width), F32),
            pltpu.VMEM((slots, tile_width, tile_width), BF16),
            pltpu.VMEM((slots, tile_width, tile_width), BF16),
            pltpu.SMEM((slots,), jnp.int32),
            pltpu.SMEM((slots,), jnp.int32),
            pltpu.SMEM((1, 1), jnp.int32),
            pltpu.VMEM((1, slots), jnp.int32),
            pltpu.VMEM((1, slots), jnp.int32),
            pltpu.VMEM((2 * vectors, width), F32),
            pltpu.VMEM((count, tile_width), F32),
            pltpu.VMEM((vectors, n_row * width), F32),
            pltpu.VMEM((vectors, n_col * width), F32),
            pltpu.VMEM((n_ct, 16, tile_width), BF16),
            pltpu.VMEM((n_rt, 16, tile_width), BF16),
            pltpu.VMEM((vectors * slots, tile_width), F32),
            pltpu.VMEM((vectors, n_rt, tile_width), F32),
            pltpu.VMEM((vectors, n_ct, tile_width), F32),
            pltpu.VMEM((vectors, n_rt // 2, tile_width), F32),
            pltpu.VMEM((3, vectors, 2 * count, tile_width), F32),
            pltpu.VMEM((vectors, 2 * count, tile_width), F32),
            pltpu.VMEM((vectors, count, tile_width), F32),
            pltpu.VMEM((2, vectors, 2 * count, tile_width), F32),
            pltpu.VMEM((2, vectors, count, tile_width), F32),
            pltpu.VMEM((vectors, count, tile_width), F32),
            pltpu.VMEM((vectors, count, tile_width), F32),
            pltpu.VMEM((vectors * count, tile_width), F32),
            pltpu.VMEM((vectors, width), F32),
            pltpu.VMEM((3, 16, 128), F32),
            pltpu.VMEM((n_col, 16, 128), F32),
            pltpu.VMEM((n_row, 16, 128), F32),
            pltpu.VMEM((2, 128), F32),
            pltpu.VMEM((n_row * n_col, 2, 128), F32),
            pltpu.VMEM((2, 128), F32),
            dma((slots // CHUNK,)),
            dma((8,)),
            dma((64,)),
            dma((n_row,)),
            dma((n_col,)),
            dma((1,)),
            dma((3,)),
            dma((2,)),
            dma((4,)),
            dma((n_col,)),
            dma((n_row,)),
            dma((2,)),
        ],
        compiler_params=pltpu.CompilerParams(
            collective_id=0, has_side_effects=True, vmem_limit_bytes=54 * 2**20
        ),
    )(
        tiles.reshape(slots, tile_width, tile_width),
        rows.reshape(slots),
        cols.reshape(slots),
        tile_counts,
        rows,
        cols,
        block_now,
        block_prev,
        diag_energy.reshape(count, tile_width),
    )
    return pl.pallas_call(
        functools.partial(finish, 1.0 / (width * n_row * n_col)),
        out_shape=(shape((vectors, width), F32), shape((8, 8), F32), shape((8, 8), F32)),
        in_specs=[vmem] * 6,
        out_specs=(vmem, vmem, vmem),
    )(shifted, early, final, block_now, block_prev, coupling)


def solution(mesh):
    return jax.shard_map(
        local,
        mesh=mesh,
        in_specs=(
            P("row", "col", None, None, None),
            P("row", "col", None),
            P("row", "col", None),
            P("row", "col"),
            P(None, ("row", "col")),
            P(None, ("row", "col")),
            P(),
            P(("row", "col")),
        ),
        out_specs=(P(None, ("row", "col")), P(), P()),
        check_vma=False,
    )
```

```python
import functools
import itertools

import jax
import jax.numpy as jnp
from jax import lax
from jax.experimental import pallas as pl
from jax.experimental.pallas import tpu as pltpu
from jax.sharding import PartitionSpec as P

MESH = pl.DeviceIdType.MESH
NT_DIMS = (((1,), (1,)), ((), ()))
NN_DIMS = (((1,), (0,)), ((), ()))
F32 = jnp.float32
BF16 = jnp.bfloat16
HIGHEST = lax.Precision.HIGHEST
CHUNK = 16
UNROLL = 64
SHIFT = 2.5


def dot_exact(left, right, dims):
    return lax.dot_general(left, right, dims, precision=HIGHEST, preferred_element_type=F32)


def split_rows(value):
    high = value.astype(BF16).astype(F32)
    return jnp.concatenate([high, value - high], axis=0).astype(BF16)


def iota(shape, axis):
    return lax.broadcasted_iota(jnp.int32, shape, axis)


def kernel(
    tiles,
    rows_h,
    cols_h,
    count_h,
    rows_w,
    cols_w,
    now_h,
    prev_h,
    diag_h,
    shifted_out,
    early_out,
    final_out,
    tile_f32,
    tile_hi,
    tile_lo,
    rows_s,
    cols_s,
    count_s,
    rows_v,
    cols_v,
    lanczos,
    diag,
    col_vec,
    row_vec,
    col_split,
    row_split,
    images,
    part_rows,
    part_cols,
    row_pair,
    row_near,
    row_far,
    row_send,
    row_last,
    col_near,
    col_far,
    col_send,
    col_last,
    image,
    shifted,
    early_send,
    early_one,
    early_two,
    final_send,
    final_all,
    final_sum,
    tile_sem,
    in_sem,
    send_sem,
    col_sem,
    row_sem,
    pair_sem,
    ring_sem,
    last_sem,
    back_sem,
    one_sem,
    two_sem,
    all_sem,
):
    r = lax.axis_index("row")
    c = lax.axis_index("col")
    z, ylo = r // 2, r % 2
    yhi, x, core = c // 8, (c // 2) % 4, c % 2
    slots = tiles.shape[0]
    width = now_h.shape[1]
    count = width // 128
    open_scope = []

    def phase(name):
        if open_scope:
            open_scope.pop().__exit__(None, None, None)
        if name:
            open_scope.append(jax.named_scope(name))
            open_scope[0].__enter__()

    def row_of(zz, yy):
        return zz * 2 + yy

    def col_of(yy, xx, cc):
        return yy * 8 + xx * 2 + cc

    zs = [(z + d) % 4 for d in (2, 1, 3)]
    xs = [(x + d) % 4 for d in (2, 1, 3)]
    row_peer = row_of(z, 1 - ylo)
    col_peer = col_of(1 - yhi, x, core)
    pair = col_of(yhi, x, 1 - core)
    zn, xn = zs[1:], xs[1:]
    across = (r, col_of(1 - yhi, xs[0], core))
    far = (row_of(zs[0], 1 - ylo), c)
    col_steps = [(2, 1), (1, 1), (3, 1), (2, 0), (0, 1), (1, 0), (3, 0)]
    col_group = [(row_of((z + a) % 4, (ylo + b) % 2), c) for a, b in col_steps]
    col_back = [(row_of((z + 4 - a) % 4, (ylo + b) % 2), c) for a, b in col_steps]

    phase("start")
    barrier = pltpu.get_barrier_semaphore()
    first_peers = [(row_peer, c), (r, col_peer), far] + [(row_of(zz, ylo), c) for zz in zs]
    first_peers += [(r, col_of(yhi, xx, core)) for xx in xs] + [(r, pair), across]
    for peer in first_peers:
        pl.semaphore_signal(barrier, inc=1, device_id=peer, device_id_type=MESH)

    now, prev = lanczos.at[0:8], lanczos.at[8:16]
    loads = [
        pltpu.make_async_copy(src, dst, in_sem.at[i])
        for i, (src, dst) in enumerate(
            [
                (now_h, now),
                (prev_h, prev),
                (diag_h, diag),
                (rows_h, rows_s),
                (cols_h, cols_s),
                (count_h, count_s),
                (rows_w, rows_v),
                (cols_w, cols_v),
            ]
        )
    ]
    loads[0].start()
    chunks = slots // CHUNK

    def tile_copy(i):
        part = pl.ds(i * CHUNK, CHUNK)
        return pltpu.make_async_copy(tiles.at[part], tile_f32.at[part], tile_sem.at[i])

    def piece(ref, p):
        return ref.at[:, pl.ds(pl.multiple_of(p * width, width), width)]

    loads[0].wait()
    for i in range(chunks):
        tile_copy(i).start()
    for copy in loads[1:]:
        copy.start()
    phase("barrier")
    pl.semaphore_wait(barrier, len(first_peers))

    sends = []
    numbers = itertools.count()

    def send(src, dst, recv, peer):
        copy = pltpu.make_async_remote_copy(
            src_ref=src,
            dst_ref=dst,
            send_sem=send_sem.at[next(numbers)],
            recv_sem=recv,
            device_id=peer,
            device_id_type=MESH,
        )
        copy.start()
        sends.append(copy)

    def arrived(dst, recv, peer):
        pltpu.make_async_remote_copy(
            src_ref=dst,
            dst_ref=dst,
            send_sem=send_sem.at[0],
            recv_sem=recv,
            device_id=peer,
            device_id_type=MESH,
        ).wait_recv()

    phase("send1")
    send(now, piece(col_vec, r), col_sem.at[r], (row_peer, c))
    send(now, piece(row_vec, c), row_sem.at[c], (r, col_peer))
    send(now, piece(col_vec, r), col_sem.at[r], far)
    for zz in zs:
        send(now, piece(col_vec, r), col_sem.at[r], (row_of(zz, ylo), c))
    for xx in xs:
        send(now, piece(row_vec, c), row_sem.at[c], (r, col_of(yhi, xx, core)))
    send(now, piece(row_vec, c), row_sem.at[c], (r, pair))
    piece(col_vec, r)[...] = now[...]
    piece(row_vec, c)[...] = now[...]

    def convert(first, last):
        def chunk(i, _):
            tile_copy(i).wait()

            def one(j, _):
                value = tile_f32[i * CHUNK + j]
                high = value.astype(BF16)
                tile_hi[i * CHUNK + j] = high
                tile_lo[i * CHUNK + j] = (value - high.astype(F32)).astype(BF16)
                return 0

            lax.fori_loop(0, CHUNK, one, 0, unroll=8)
            return 0

        lax.fori_loop(first, last, chunk, 0)

    phase("conv1")
    convert(0, 9)
    phase("fwdrow")
    arrived(piece(col_vec, row_peer), col_sem.at[row_peer], (row_peer, c))
    for zz in zn:
        send(
            piece(col_vec, row_peer), piece(col_vec, row_peer), col_sem.at[row_peer], (row_of(zz, ylo), c)
        )
    phase("fwdcol")
    arrived(piece(row_vec, col_peer), row_sem.at[col_peer], (r, col_peer))
    for xx in xs:
        send(
            piece(row_vec, col_peer),
            piece(row_vec, col_peer),
            row_sem.at[col_peer],
            (r, col_of(yhi, xx, core)),
        )
    send(piece(row_vec, col_peer), piece(row_vec, col_peer), row_sem.at[col_peer], (r, pair))
    phase("conv2")
    convert(9, chunks)
    for copy in loads[1:]:
        copy.wait()
    phase("early")
    early_send[...] = jnp.zeros_like(early_send)
    known = lanczos[...]
    early_send[0, :, 0:16] = dot_exact(known, known, NT_DIMS)

    phase("waitcolvec")
    for zz in zn:
        for yy in (ylo, 1 - ylo):
            p = row_of(zz, yy)
            arrived(piece(col_vec, p), col_sem.at[p], (row_of(zz, ylo), c))
    for p in (row_of(zs[0], ylo), far[0]):
        arrived(piece(col_vec, p), col_sem.at[p], (p, c))

    def split_vectors(src, dst):
        def one(t, _):
            dst[t] = split_rows(src[:, pl.ds(pl.multiple_of(t * 128, 128), 128)])
            return 0

        lax.fori_loop(0, dst.shape[0], one, 0, unroll=16)

    phase("split1")
    split_vectors(col_vec, col_split)

    def products(first, last, index, vectors, transposed):
        def body(g, _):
            for u in range(UNROLL):
                m = g * UNROLL + u
                left = vectors[index[m]]
                if transposed:
                    weights = jnp.concatenate([tile_hi[m], tile_lo[m]], axis=0)
                    out = lax.dot_general(left, weights, NT_DIMS, preferred_element_type=F32)
                else:
                    weights = jnp.concatenate([tile_hi[m], tile_lo[m]], axis=1)
                    out = lax.dot_general(left, weights, NN_DIMS, preferred_element_type=F32)
                total = (out[0:8, 0:128] + out[8:16, 0:128]) + out[0:8, 128:256]
                images[pl.ds(m, 8, stride=slots), :] = total
            return 0

        lax.fori_loop(first // UNROLL, last // UNROLL, body, 0)

    used = iota((1, slots), 1) < count_s[0, 0]

    def scatter(place, dst):
        wanted = jnp.where(used, place, -1)
        pick = (iota((dst.shape[1], slots), 0) == wanted).astype(F32).astype(BF16)
        for v in range(8):
            value = images[v * slots : (v + 1) * slots, :]
            high = value.astype(BF16)
            low = (value - high.astype(F32)).astype(BF16)
            out = lax.dot_general(
                pick, jnp.concatenate([high, low], axis=1), NN_DIMS, preferred_element_type=F32
            )
            dst[v] = out[:, 0:128] + out[:, 128:256]

    phase("prodrows1")
    products(0, 2 * UNROLL, cols_s, col_split, True)
    phase("relay")
    for yy in (yhi, 1 - yhi):
        for xx in xs:
            p = col_of(yy, xx, core)
            arrived(piece(row_vec, p), row_sem.at[p], (r, col_of(yhi, xx, core)))
            send(piece(row_vec, p), piece(row_vec, p), row_sem.at[p], (r, pair))
    phase("prodrows2")
    products(2 * UNROLL, slots, cols_s, col_split, True)
    phase("scatrows")
    place = rows_v[...]
    owner = place // 16
    scatter(
        ((owner % 2) * 8 + ((owner // 2) % 4) * 2 + owner // 8) * 16 + place % 16, part_rows
    )
    half = part_rows.shape[1] // 2

    def half_of(cc):
        return part_rows.at[:, pl.ds(pl.multiple_of(cc * half, half), half), :]

    send(half_of(1 - core), row_pair, pair_sem.at[0], (r, pair))

    phase("waitrowvec")
    for yy in (yhi, 1 - yhi):
        for xx in [x] + xs:
            p = col_of(yy, xx, 1 - core)
            arrived(piece(row_vec, p), row_sem.at[p], (r, pair))
    row_steps = list(itertools.product(range(2), range(4), range(2)))[1:]
    row_group = [(r, col_of((yhi + a) % 2, (x + b) % 4, (core + d) % 2)) for a, b, d in row_steps]
    row_back = [
        (r, col_of((yhi + a) % 2, (x + 4 - b) % 4, (core + d) % 2)) for a, b, d in row_steps
    ]
    phase("split2")
    split_vectors(row_vec, row_split)
    phase("prodcols1")
    products(0, UNROLL, rows_s, row_split, False)
    phase("waitpair")
    arrived(row_pair, pair_sem.at[0], (r, pair))
    mine = half_of(core)
    for v in range(8):
        row_pair[v] = row_pair[v] + mine[v]
    for d, xx in enumerate(xn):
        send(
            row_pair.at[:, pl.ds(pl.multiple_of(xx * 2 * count, 2 * count), 2 * count), :],
            row_near.at[d],
            ring_sem.at[d],
            (r, col_of(yhi, xx, core)),
        )
    early_one[c] = early_send[0]
    for peer in row_group:
        send(early_send.at[0], early_one.at[c], one_sem.at[c], peer)
    phase("prodcols2")
    products(UNROLL, 3 * UNROLL, rows_s, row_split, False)
    phase("rowfar")
    opposite = xs[0] * 2 * count
    for d, (yy, peer) in enumerate([(1 - yhi, across), (yhi, (r, col_of(yhi, xs[0], core)))]):
        send(
            row_pair.at[:, pl.ds(pl.multiple_of(opposite + yy * count, count), count), :],
            row_far.at[d],
            ring_sem.at[2 + d],
            peer,
        )
    phase("prodcols3")
    products(3 * UNROLL, slots, rows_s, row_split, False)
    phase("scatcols")
    scatter(cols_v[...], part_cols)

    def lot(ref, k):
        return ref.at[:, pl.ds(pl.multiple_of(k * count, count), count), :]

    for d, zz in enumerate(zn):
        send(
            part_cols.at[:, pl.ds(pl.multiple_of(zz * 2 * count, 2 * count), 2 * count), :],
            col_near.at[d],
            back_sem.at[d],
            (row_of(zz, ylo), c),
        )
    phase("rownear")
    for d in range(2):
        arrived(row_near.at[d], ring_sem.at[d], (r, col_of(yhi, xn[1 - d], core)))
    mine_at = pl.multiple_of(x * 2 * count + yhi * count, count)
    away_at = pl.multiple_of(x * 2 * count + (1 - yhi) * count, count)
    for v in range(8):
        at = pl.ds(pl.multiple_of((1 - yhi) * count, count), count)
        row_send[v] = row_pair[v, pl.ds(away_at, count), :] + (row_near[0, v, at, :] + row_near[1, v, at, :])
    send(row_send, row_last, last_sem.at[0], (r, col_peer))
    phase("colfar")
    send(lot(part_cols, far[0]), col_far.at[0], back_sem.at[2], far)
    send(
        lot(part_cols, row_of(zs[0], ylo)), col_far.at[1], back_sem.at[3], (row_of(zs[0], ylo), c)
    )
    phase("near")
    for d in range(2):
        arrived(col_near.at[d], back_sem.at[d], (row_of(zn[1 - d], ylo), c))
    at = pl.multiple_of((1 - ylo) * count, count)
    away = lot(part_cols, row_peer)
    for v in range(8):
        col_send[v] = away[v] + (col_near[0, v, pl.ds(at, count), :] + col_near[1, v, pl.ds(at, count), :])
    send(col_send, col_last, last_sem.at[1], (row_peer, c))

    phase("waitfar")
    arrived(row_far.at[0], ring_sem.at[2], across)
    arrived(row_far.at[1], ring_sem.at[3], (r, col_of(yhi, xs[0], core)))
    arrived(col_far.at[0], back_sem.at[2], far)
    arrived(col_far.at[1], back_sem.at[3], (row_of(zs[0], ylo), c))
    home = pl.ds(pl.multiple_of(ylo * count, count), count)
    own = pl.ds(pl.multiple_of(yhi * count, count), count)
    col_mine = lot(part_cols, r)
    for v in range(8):
        total = (row_pair[v, pl.ds(mine_at, count), :] + col_mine[v]) + (col_far[0, v] + col_far[1, v])
        total = total + (row_far[0, v] + row_far[1, v])
        total = total + (row_near[0, v, own, :] + row_near[1, v, own, :])
        image[v * count : (v + 1) * count, :] = total + (col_near[0, v, home, :] + col_near[1, v, home, :])
    phase("early1")
    for peer in row_back:
        arrived(early_one.at[peer[1]], one_sem.at[peer[1]], peer)
    total = early_one[0]
    for i in range(1, early_one.shape[0]):
        total = total + early_one[i]
    early_send[1] = total
    early_two[r] = total
    for peer in col_group:
        send(early_send.at[1], early_two.at[r], two_sem.at[r], peer)
    phase("waitlast")
    arrived(col_last, last_sem.at[1], (row_peer, c))
    arrived(row_last, last_sem.at[0], (r, col_peer))
    phase("shifted")
    for v in range(8):
        part = slice(v * count, (v + 1) * count)
        image[part, :] = image[part, :] + (row_last[v] + col_last[v])
    for t in range(count):
        at = slice(t * 128, (t + 1) * 128)
        shifted[:, at] = image[pl.ds(t, 8, stride=count), :] + (diag[t : t + 1, :] - SHIFT) * now[:, at]
    shifted_copy = pltpu.make_async_copy(shifted, shifted_out, in_sem.at[0])
    shifted_copy.start()

    phase("gram")
    value = shifted[...]
    gram = dot_exact(value, jnp.concatenate([value, lanczos[...]], axis=0), NT_DIMS)
    place, lane = iota((24, 256), 0), iota((24, 256), 1)
    spread = ((lane // 64 == place // 8) & (lane % 8 == place % 8)).astype(F32)
    flat = dot_exact(gram, spread, NN_DIMS)
    flat = jnp.where((iota((8, 256), 1) // 8) % 8 == iota((8, 256), 0), flat, 0.0)
    flat = jnp.sum(flat, axis=0, keepdims=True)
    final_send[0:1, :] = flat[:, 0:128]
    final_send[1:2, :] = flat[:, 128:256]
    phase("final")
    me = r * early_one.shape[0] + c
    own_copy = pltpu.make_async_copy(final_send, final_all.at[me], in_sem.at[2])
    own_copy.start()
    steps = sorted(
        itertools.product(range(4), range(2), range(2), range(4), range(2)),
        key=lambda s: -(min(s[0], 4 - s[0]) + s[1] + 2 * s[2] + min(s[3], 4 - s[3])),
    )
    steps.remove((0, 0, 0, 0, 0))
    lasts = []
    for a, b, d, e, f in steps:
        peer = (
            row_of((z + a) % 4, (ylo + b) % 2),
            col_of((yhi + d) % 2, (x + e) % 4, (core + f) % 2),
        )
        copy = pltpu.make_async_remote_copy(
            src_ref=final_send,
            dst_ref=final_all.at[me],
            send_sem=all_sem.at[0],
            recv_sem=all_sem.at[1],
            device_id=peer,
            device_id_type=MESH,
        )
        copy.start()
        lasts.append(peer)
    phase("early2")
    for peer in col_back:
        arrived(early_two.at[peer[0]], two_sem.at[peer[0]], peer)
    total = early_two[0]
    for i in range(1, early_two.shape[0]):
        total = total + early_two[i]
    early_send[2] = total
    early_copy = pltpu.make_async_copy(early_send.at[2], early_out, in_sem.at[1])
    early_copy.start()

    phase("waitfinal")
    own_copy.wait()
    others = final_all.at[0 : len(steps)]
    waiter = pltpu.make_async_remote_copy(
        src_ref=others,
        dst_ref=others,
        send_sem=all_sem.at[0],
        recv_sem=all_sem.at[1],
        device_id=lasts[0],
        device_id_type=MESH,
    )
    waiter.wait_recv()
    phase("sum")
    final_sum[...] = jnp.sum(final_all[...], axis=0)
    final_copy = pltpu.make_async_copy(final_sum, final_out, in_sem.at[2])
    final_copy.start()
    phase("waitsends")
    for copy in sends:
        copy.wait_send()
    waiter.wait_send()
    shifted_copy.wait()
    early_copy.wait()
    final_copy.wait()
    phase(None)


def finish(scale, shifted, early, final, now, prev, coupling, next_out, alpha_out, beta_out):
    open_scope = []

    def phase(name):
        if open_scope:
            open_scope.pop().__exit__(None, None, None)
        if name:
            open_scope.append(jax.named_scope(name))
            open_scope[0].__enter__()

    phase("Bgram")
    line, lane = iota((8, 16), 0), iota((8, 16), 1)
    flat = jnp.concatenate([final[0:1, :], final[1:2, :]], axis=1) * scale
    flat = jnp.where((iota((8, 256), 1) // 8) % 8 == iota((8, 256), 0), flat, 0.0)
    high = flat.astype(BF16)
    rest = flat - high.astype(F32)
    mid = rest.astype(BF16)
    low = (rest - mid.astype(F32)).astype(BF16)
    parts = jnp.concatenate([high.astype(F32), mid.astype(F32), low.astype(F32)], axis=0).astype(BF16)
    place, at = iota((16, 256), 0), iota((16, 256), 1)

    def gathered(block):
        pick = ((at // 64 == block) & (at % 8 == place % 8)).astype(F32).astype(BF16)
        out = lax.dot_general(parts, pick, NT_DIMS, preferred_element_type=F32)
        return (out[0:8] + out[8:16]) + out[16:24]

    cross = gathered(1 + place // 8)
    square = gathered(jnp.where(place < 8, 0, -1))
    known = early[:, 0:16] * scale
    eye = (line == lane).astype(F32)
    shift_eye = (line + 8 == lane).astype(F32)
    coupled = dot_exact(coupling[...], shift_eye, NN_DIMS)
    alpha_t = cross + SHIFT * known[0:8]
    weights = jnp.where(lane < 8, SHIFT * eye - alpha_t, -coupled)
    zeros = jnp.zeros((8, 16), F32)
    mixed = cross + 0.5 * dot_exact(weights, known, NN_DIMS)
    once = dot_exact(mixed, jnp.concatenate([weights, zeros], axis=0), NT_DIMS)
    again = dot_exact(weights, jnp.concatenate([mixed, zeros], axis=0), NT_DIMS)
    residual = shifted[...] + dot_exact(
        weights, jnp.concatenate([now[...], prev[...]], axis=0), NN_DIMS
    )
    phase("Bchol")
    gram = square + (once + again)

    def entry(a, b):
        return jnp.broadcast_to(gram[a : a + 1, b : b + 1], (8, 128))

    upper = {(a, b): entry(a, b) for a in range(8) for b in range(a, 8)}
    inverse = {}
    for a in range(8):
        pivot = 1.0 / upper[a, a]
        for b in range(a + 1, 8):
            factor = upper[a, b] * pivot
            for k in range(b, 8):
                upper[b, k] = upper[b, k] - factor * upper[a, k]
            for k in range(a):
                inverse[b, k] = inverse[b, k] - factor * inverse[a, k]
            inverse[b, a] = -factor
    line, lane = iota((8, 128), 0), iota((8, 128), 1)
    solve = jnp.zeros((8, 128), F32)
    beta = jnp.zeros((8, 128), F32)
    for a in range(8):
        root = jnp.sqrt(upper[a, a])
        scale_row = 1.0 / root
        solve = jnp.where((line == a) & (lane == a), scale_row, solve)
        beta = jnp.where((line == a) & (lane == a), root, beta)
        for k in range(a):
            solve = jnp.where((line == a) & (lane == k), inverse[a, k] * scale_row, solve)
        for b in range(a + 1, 8):
            beta = jnp.where((line == a) & (lane == b), upper[a, b] * scale_row, beta)
    phase("Bsolve")
    next_out[...] = dot_exact(solve[:, 0:8], residual, NN_DIMS)
    beta_out[...] = beta[:, 0:8]
    alpha_out[...] = dot_exact(eye[:, 0:8], alpha_t[:, 0:8], NT_DIMS)
    phase(None)


def local(tiles, tile_rows, tile_cols, tile_counts, block_now, block_prev, coupling, diag_energy):
    slots, tile_width = tiles.shape[2], tiles.shape[3]
    vectors, width = block_now.shape
    n_row, n_col = lax.axis_size("row"), lax.axis_size("col")
    count = width // tile_width
    rows, cols = tile_rows.reshape(1, slots), tile_cols.reshape(1, slots)
    hbm = pl.BlockSpec(memory_space=pltpu.HBM)
    vmem = pl.BlockSpec(memory_space=pltpu.VMEM)
    dma = pltpu.SemaphoreType.DMA
    n_rt, n_ct = n_col * count, n_row * count
    shape = jax.ShapeDtypeStruct
    shifted, early, final = pl.pallas_call(
        kernel,
        out_shape=(shape((vectors, width), F32), shape((16, 128), F32), shape((2, 128), F32)),
        in_specs=[hbm] * 9,
        out_specs=(hbm, hbm, hbm),
        scratch_shapes=[
            pltpu.VMEM((slots, tile_width, tile_width), F32),
            pltpu.VMEM((slots, tile_width, tile_width), BF16),
            pltpu.VMEM((slots, tile_width, tile_width), BF16),
            pltpu.SMEM((slots,), jnp.int32),
            pltpu.SMEM((slots,), jnp.int32),
            pltpu.SMEM((1, 1), jnp.int32),
            pltpu.VMEM((1, slots), jnp.int32),
            pltpu.VMEM((1, slots), jnp.int32),
            pltpu.VMEM((2 * vectors, width), F32),
            pltpu.VMEM((count, tile_width), F32),
            pltpu.VMEM((vectors, n_row * width), F32),
            pltpu.VMEM((vectors, n_col * width), F32),
            pltpu.VMEM((n_ct, 16, tile_width), BF16),
            pltpu.VMEM((n_rt, 16, tile_width), BF16),
            pltpu.VMEM((vectors * slots, tile_width), F32),
            pltpu.VMEM((vectors, n_rt, tile_width), F32),
            pltpu.VMEM((vectors, n_ct, tile_width), F32),
            pltpu.VMEM((vectors, n_rt // 2, tile_width), F32),
            pltpu.VMEM((2, vectors, 2 * count, tile_width), F32),
            pltpu.VMEM((2, vectors, count, tile_width), F32),
            pltpu.VMEM((vectors, count, tile_width), F32),
            pltpu.VMEM((vectors, count, tile_width), F32),
            pltpu.VMEM((2, vectors, 2 * count, tile_width), F32),
            pltpu.VMEM((2, vectors, count, tile_width), F32),
            pltpu.VMEM((vectors, count, tile_width), F32),
            pltpu.VMEM((vectors, count, tile_width), F32),
            pltpu.VMEM((vectors * count, tile_width), F32),
            pltpu.VMEM((vectors, width), F32),
            pltpu.VMEM((3, 16, 128), F32),
            pltpu.VMEM((n_col, 16, 128), F32),
            pltpu.VMEM((n_row, 16, 128), F32),
            pltpu.VMEM((2, 128), F32),
            pltpu.VMEM((n_row * n_col, 2, 128), F32),
            pltpu.VMEM((2, 128), F32),
            dma((slots // CHUNK,)),
            dma((8,)),
            dma((64,)),
            dma((n_row,)),
            dma((n_col,)),
            dma((1,)),
            dma((4,)),
            dma((2,)),
            dma((4,)),
            dma((n_col,)),
            dma((n_row,)),
            dma((2,)),
        ],
        compiler_params=pltpu.CompilerParams(
            collective_id=0, has_side_effects=True, vmem_limit_bytes=54 * 2**20
        ),
    )(
        tiles.reshape(slots, tile_width, tile_width),
        rows.reshape(slots),
        cols.reshape(slots),
        tile_counts,
        rows,
        cols,
        block_now,
        block_prev,
        diag_energy.reshape(count, tile_width),
    )
    return pl.pallas_call(
        functools.partial(finish, 1.0 / (width * n_row * n_col)),
        out_shape=(shape((vectors, width), F32), shape((8, 8), F32), shape((8, 8), F32)),
        in_specs=[vmem] * 6,
        out_specs=(vmem, vmem, vmem),
    )(shifted, early, final, block_now, block_prev, coupling)


def solution(mesh):
    return jax.shard_map(
        local,
        mesh=mesh,
        in_specs=(
            P("row", "col", None, None, None),
            P("row", "col", None),
            P("row", "col", None),
            P("row", "col"),
            P(None, ("row", "col")),
            P(None, ("row", "col")),
            P(),
            P(("row", "col")),
        ),
        out_specs=(P(None, ("row", "col")), P(), P()),
        check_vma=False,
    )
```

```python
import functools
import itertools

import jax
import jax.numpy as jnp
from jax import lax
from jax.experimental import pallas as pl
from jax.experimental.pallas import tpu as pltpu
from jax.sharding import PartitionSpec as P

MESH = pl.DeviceIdType.MESH
NT_DIMS = (((1,), (1,)), ((), ()))
NN_DIMS = (((1,), (0,)), ((), ()))
F32 = jnp.float32
BF16 = jnp.bfloat16
HIGHEST = lax.Precision.HIGHEST
CHUNK = 16
UNROLL = 64
SHIFT = 2.5


def dot_exact(left, right, dims):
    return lax.dot_general(left, right, dims, precision=HIGHEST, preferred_element_type=F32)


def split_rows(value):
    high = value.astype(BF16).astype(F32)
    return jnp.concatenate([high, value - high], axis=0).astype(BF16)


def three_parts(value):
    high = value.astype(BF16).astype(F32)
    mid = (value - high).astype(BF16).astype(F32)
    return jnp.concatenate([high, mid, (value - high) - mid], axis=0).astype(BF16)


def iota(shape, axis):
    return lax.broadcasted_iota(jnp.int32, shape, axis)


def kernel(
    tiles,
    rows_h,
    cols_h,
    count_h,
    rows_w,
    cols_w,
    now_h,
    prev_h,
    diag_h,
    shifted,
    early_out,
    final_out,
    tile_f32,
    tile_hi,
    tile_lo,
    rows_s,
    cols_s,
    count_s,
    rows_v,
    cols_v,
    lanczos,
    diag,
    col_vec,
    row_vec,
    col_split,
    row_split,
    images,
    part_rows,
    part_cols,
    row_pair,
    row_near,
    row_far,
    row_send,
    row_last,
    col_near,
    col_far,
    col_send,
    col_last,
    image,
    early_send,
    early_one,
    early_two,
    final_send,
    final_all,
    known_split,
    tile_sem,
    in_sem,
    send_sem,
    col_sem,
    row_sem,
    pair_sem,
    ring_sem,
    last_sem,
    back_sem,
    one_sem,
    two_sem,
    all_sem,
):
    r = lax.axis_index("row")
    c = lax.axis_index("col")
    z, ylo = r // 2, r % 2
    yhi, x, core = c // 8, (c // 2) % 4, c % 2
    slots = tiles.shape[0]
    width = now_h.shape[1]
    count = width // 128
    open_scope = []

    def phase(name):
        if open_scope:
            open_scope.pop().__exit__(None, None, None)
        if name:
            open_scope.append(jax.named_scope(name))
            open_scope[0].__enter__()

    def row_of(zz, yy):
        return zz * 2 + yy

    def col_of(yy, xx, cc):
        return yy * 8 + xx * 2 + cc

    zs = [(z + d) % 4 for d in (2, 1, 3)]
    xs = [(x + d) % 4 for d in (2, 1, 3)]
    row_peer = row_of(z, 1 - ylo)
    col_peer = col_of(1 - yhi, x, core)
    pair = col_of(yhi, x, 1 - core)
    zn, xn = zs[1:], xs[1:]
    across = (r, col_of(1 - yhi, xs[0], core))
    far = (row_of(zs[0], 1 - ylo), c)
    col_steps = [(2, 1), (1, 1), (3, 1), (2, 0), (0, 1), (1, 0), (3, 0)]
    col_group = [(row_of((z + a) % 4, (ylo + b) % 2), c) for a, b in col_steps]
    col_back = [(row_of((z + 4 - a) % 4, (ylo + b) % 2), c) for a, b in col_steps]

    phase("start")
    barrier = pltpu.get_barrier_semaphore()
    first_peers = [(row_peer, c), (r, col_peer), far] + [(row_of(zz, ylo), c) for zz in zs]
    first_peers += [(r, col_of(yhi, xx, core)) for xx in xs] + [(r, pair), across]
    for peer in first_peers:
        pl.semaphore_signal(barrier, inc=1, device_id=peer, device_id_type=MESH)

    now, prev = lanczos.at[0:8], lanczos.at[8:16]
    loads = [
        pltpu.make_async_copy(src, dst, in_sem.at[i])
        for i, (src, dst) in enumerate(
            [
                (now_h, now),
                (prev_h, prev),
                (diag_h, diag),
                (rows_h, rows_s),
                (cols_h, cols_s),
                (count_h, count_s),
                (rows_w, rows_v),
                (cols_w, cols_v),
            ]
        )
    ]
    loads[0].start()
    chunks = slots // CHUNK

    def tile_copy(i):
        part = pl.ds(i * CHUNK, CHUNK)
        return pltpu.make_async_copy(tiles.at[part], tile_f32.at[part], tile_sem.at[i])

    def piece(ref, p):
        return ref.at[:, pl.ds(pl.multiple_of(p * width, width), width)]

    loads[0].wait()
    for i in range(chunks):
        tile_copy(i).start()
    for copy in loads[1:]:
        copy.start()
    phase("barrier")
    pl.semaphore_wait(barrier, len(first_peers))

    sends = []
    numbers = itertools.count()

    def send(src, dst, recv, peer):
        copy = pltpu.make_async_remote_copy(
            src_ref=src,
            dst_ref=dst,
            send_sem=send_sem.at[next(numbers)],
            recv_sem=recv,
            device_id=peer,
            device_id_type=MESH,
        )
        copy.start()
        sends.append(copy)

    def arrived(dst, recv, peer):
        pltpu.make_async_remote_copy(
            src_ref=dst,
            dst_ref=dst,
            send_sem=send_sem.at[0],
            recv_sem=recv,
            device_id=peer,
            device_id_type=MESH,
        ).wait_recv()

    phase("send1")
    send(now, piece(col_vec, r), col_sem.at[r], (row_peer, c))
    send(now, piece(row_vec, c), row_sem.at[c], (r, col_peer))
    send(now, piece(col_vec, r), col_sem.at[r], far)
    for zz in zs:
        send(now, piece(col_vec, r), col_sem.at[r], (row_of(zz, ylo), c))
    for xx in xs:
        send(now, piece(row_vec, c), row_sem.at[c], (r, col_of(yhi, xx, core)))
    send(now, piece(row_vec, c), row_sem.at[c], (r, pair))
    piece(col_vec, r)[...] = now[...]
    piece(row_vec, c)[...] = now[...]

    def convert(first, last):
        def chunk(i, _):
            tile_copy(i).wait()

            def one(j, _):
                value = tile_f32[i * CHUNK + j]
                high = value.astype(BF16)
                tile_hi[i * CHUNK + j] = high
                tile_lo[i * CHUNK + j] = (value - high.astype(F32)).astype(BF16)
                return 0

            lax.fori_loop(0, CHUNK, one, 0, unroll=8)
            return 0

        lax.fori_loop(first, last, chunk, 0)

    phase("conv1")
    convert(0, 9)
    phase("fwdrow")
    arrived(piece(col_vec, row_peer), col_sem.at[row_peer], (row_peer, c))
    for zz in zn:
        send(
            piece(col_vec, row_peer), piece(col_vec, row_peer), col_sem.at[row_peer], (row_of(zz, ylo), c)
        )
    phase("fwdcol")
    arrived(piece(row_vec, col_peer), row_sem.at[col_peer], (r, col_peer))
    for xx in xs:
        send(
            piece(row_vec, col_peer),
            piece(row_vec, col_peer),
            row_sem.at[col_peer],
            (r, col_of(yhi, xx, core)),
        )
    send(piece(row_vec, col_peer), piece(row_vec, col_peer), row_sem.at[col_peer], (r, pair))
    phase("conv2")
    convert(9, chunks)
    for copy in loads[1:]:
        copy.wait()
    phase("early")
    early_send[...] = jnp.zeros_like(early_send)
    known = lanczos[...]
    high = known.astype(BF16)
    known_split[0] = high
    known_split[1] = (known - high.astype(F32)).astype(BF16)
    early_send[0, :, 0:16] = dot_exact(known, known, NT_DIMS)

    phase("waitcolvec")
    for zz in zn:
        for yy in (ylo, 1 - ylo):
            p = row_of(zz, yy)
            arrived(piece(col_vec, p), col_sem.at[p], (row_of(zz, ylo), c))
    for p in (row_of(zs[0], ylo), far[0]):
        arrived(piece(col_vec, p), col_sem.at[p], (p, c))

    def split_vectors(src, dst):
        def one(t, _):
            dst[t] = split_rows(src[:, pl.ds(pl.multiple_of(t * 128, 128), 128)])
            return 0

        lax.fori_loop(0, dst.shape[0], one, 0, unroll=16)

    phase("split1")
    split_vectors(col_vec, col_split)

    def products(first, last, index, vectors, transposed):
        for m in range(first, last):
            left = vectors[index[m]]
            if transposed:
                weights = jnp.concatenate([tile_hi[m], tile_lo[m]], axis=0)
                out = lax.dot_general(left, weights, NT_DIMS, preferred_element_type=F32)
            else:
                weights = jnp.concatenate([tile_hi[m], tile_lo[m]], axis=1)
                out = lax.dot_general(left, weights, NN_DIMS, preferred_element_type=F32)
            total = (out[0:8, 0:128] + out[8:16, 0:128]) + out[0:8, 128:256]
            images[pl.ds(m, 8, stride=slots), :] = total

    used = iota((1, slots), 1) < count_s[0, 0]

    def scatter(place, dst):
        wanted = jnp.where(used, place, -1)
        pick = (iota((dst.shape[1], slots), 0) == wanted).astype(F32).astype(BF16)
        for v in range(8):
            value = images[v * slots : (v + 1) * slots, :]
            high = value.astype(BF16)
            low = (value - high.astype(F32)).astype(BF16)
            out = lax.dot_general(
                pick, jnp.concatenate([high, low], axis=1), NN_DIMS, preferred_element_type=F32
            )
            dst[v] = out[:, 0:128] + out[:, 128:256]

    phase("prodrows1")
    products(0, 2 * UNROLL, cols_s, col_split, True)
    phase("relay")
    for yy in (yhi, 1 - yhi):
        for xx in xs:
            p = col_of(yy, xx, core)
            arrived(piece(row_vec, p), row_sem.at[p], (r, col_of(yhi, xx, core)))
            send(piece(row_vec, p), piece(row_vec, p), row_sem.at[p], (r, pair))
    phase("prodrows2")
    products(2 * UNROLL, slots, cols_s, col_split, True)
    phase("scatrows")
    place = rows_v[...]
    owner = place // 16
    scatter(
        ((owner % 2) * 8 + ((owner // 2) % 4) * 2 + owner // 8) * 16 + place % 16, part_rows
    )
    half = part_rows.shape[1] // 2

    def half_of(cc):
        return part_rows.at[:, pl.ds(pl.multiple_of(cc * half, half), half), :]

    send(half_of(1 - core), row_pair, pair_sem.at[0], (r, pair))

    phase("waitrowvec")
    for yy in (yhi, 1 - yhi):
        for xx in [x] + xs:
            p = col_of(yy, xx, 1 - core)
            arrived(piece(row_vec, p), row_sem.at[p], (r, pair))
    row_steps = list(itertools.product(range(2), range(4), range(2)))[1:]
    row_group = [(r, col_of((yhi + a) % 2, (x + b) % 4, (core + d) % 2)) for a, b, d in row_steps]
    row_back = [
        (r, col_of((yhi + a) % 2, (x + 4 - b) % 4, (core + d) % 2)) for a, b, d in row_steps
    ]
    phase("split2")
    split_vectors(row_vec, row_split)
    phase("prodcols1")
    products(0, UNROLL, rows_s, row_split, False)
    phase("waitpair")
    arrived(row_pair, pair_sem.at[0], (r, pair))
    mine = half_of(core)
    for v in range(8):
        row_pair[v] = row_pair[v] + mine[v]
    for d, xx in enumerate(xn):
        send(
            row_pair.at[:, pl.ds(pl.multiple_of(xx * 2 * count, 2 * count), 2 * count), :],
            row_near.at[d],
            ring_sem.at[d],
            (r, col_of(yhi, xx, core)),
        )
    early_one[c] = early_send[0]
    for peer in row_group:
        send(early_send.at[0], early_one.at[c], one_sem.at[c], peer)
    phase("prodcols2")
    products(UNROLL, 3 * UNROLL, rows_s, row_split, False)
    phase("rowfar")
    opposite = xs[0] * 2 * count
    for d, (yy, peer) in enumerate([(1 - yhi, across), (yhi, (r, col_of(yhi, xs[0], core)))]):
        send(
            row_pair.at[:, pl.ds(pl.multiple_of(opposite + yy * count, count), count), :],
            row_far.at[d],
            ring_sem.at[2 + d],
            peer,
        )
    phase("prodcols3")
    products(3 * UNROLL, slots, rows_s, row_split, False)
    phase("scatcols")
    scatter(cols_v[...], part_cols)

    def lot(ref, k):
        return ref.at[:, pl.ds(pl.multiple_of(k * count, count), count), :]

    for d, zz in enumerate(zn):
        send(
            part_cols.at[:, pl.ds(pl.multiple_of(zz * 2 * count, 2 * count), 2 * count), :],
            col_near.at[d],
            back_sem.at[d],
            (row_of(zz, ylo), c),
        )
    phase("rownear")
    for d in range(2):
        arrived(row_near.at[d], ring_sem.at[d], (r, col_of(yhi, xn[1 - d], core)))
    mine_at = pl.multiple_of(x * 2 * count + yhi * count, count)
    away_at = pl.multiple_of(x * 2 * count + (1 - yhi) * count, count)
    for v in range(8):
        at = pl.ds(pl.multiple_of((1 - yhi) * count, count), count)
        row_send[v] = row_pair[v, pl.ds(away_at, count), :] + (row_near[0, v, at, :] + row_near[1, v, at, :])
    send(row_send, row_last, last_sem.at[0], (r, col_peer))
    phase("colfar")
    send(lot(part_cols, far[0]), col_far.at[0], back_sem.at[2], far)
    send(
        lot(part_cols, row_of(zs[0], ylo)), col_far.at[1], back_sem.at[3], (row_of(zs[0], ylo), c)
    )
    phase("near")
    for d in range(2):
        arrived(col_near.at[d], back_sem.at[d], (row_of(zn[1 - d], ylo), c))
    at = pl.multiple_of((1 - ylo) * count, count)
    away = lot(part_cols, row_peer)
    for v in range(8):
        col_send[v] = away[v] + (col_near[0, v, pl.ds(at, count), :] + col_near[1, v, pl.ds(at, count), :])
    send(col_send, col_last, last_sem.at[1], (row_peer, c))

    phase("waitfar")
    arrived(row_far.at[0], ring_sem.at[2], across)
    arrived(row_far.at[1], ring_sem.at[3], (r, col_of(yhi, xs[0], core)))
    arrived(col_far.at[0], back_sem.at[2], far)
    arrived(col_far.at[1], back_sem.at[3], (row_of(zs[0], ylo), c))
    home = pl.ds(pl.multiple_of(ylo * count, count), count)
    own = pl.ds(pl.multiple_of(yhi * count, count), count)
    col_mine = lot(part_cols, r)
    for v in range(8):
        total = (row_pair[v, pl.ds(mine_at, count), :] + col_mine[v]) + (col_far[0, v] + col_far[1, v])
        total = total + (row_far[0, v] + row_far[1, v])
        total = total + (row_near[0, v, own, :] + row_near[1, v, own, :])
        image[v * count : (v + 1) * count, :] = total + (col_near[0, v, home, :] + col_near[1, v, home, :])
    phase("early1")
    for peer in row_back:
        arrived(early_one.at[peer[1]], one_sem.at[peer[1]], peer)
    total = early_one[0]
    for i in range(1, early_one.shape[0]):
        total = total + early_one[i]
    early_send[1] = total
    early_two[r] = total
    for peer in col_group:
        send(early_send.at[1], early_two.at[r], two_sem.at[r], peer)
    phase("waitlast")
    arrived(col_last, last_sem.at[1], (row_peer, c))
    arrived(row_last, last_sem.at[0], (r, col_peer))
    phase("shifted")
    for v in range(8):
        part = slice(v * count, (v + 1) * count)
        image[part, :] = image[part, :] + (row_last[v] + col_last[v])
    for t in range(count):
        at = slice(t * 128, (t + 1) * 128)
        shifted[:, at] = image[pl.ds(t, 8, stride=count), :] + (diag[t : t + 1, :] - SHIFT) * now[:, at]

    phase("gram")
    halves = split_rows(shifted[...])
    gram = lax.dot_general(
        halves,
        jnp.concatenate([halves, known_split[0], known_split[1]], axis=0),
        NT_DIMS,
        preferred_element_type=F32,
    )
    gram = gram[0:8] + gram[8:16]
    place, lane = iota((48, 256), 0), iota((48, 256), 1)
    block = jnp.where(place < 16, 0, 1 + (place // 8) % 2)
    spread = ((lane // 64 == block) & (lane % 8 == place % 8)).astype(F32).astype(BF16)
    flat = lax.dot_general(three_parts(gram), spread, NN_DIMS, preferred_element_type=F32)
    flat = (flat[0:8] + flat[8:16]) + flat[16:24]
    flat = jnp.where((iota((8, 256), 1) // 8) % 8 == iota((8, 256), 0), flat, 0.0)
    flat = jnp.sum(flat, axis=0, keepdims=True)
    final_send[0:1, :] = flat[:, 0:128]
    final_send[1:2, :] = flat[:, 128:256]
    phase("final")
    me = r * early_one.shape[0] + c
    own_copy = pltpu.make_async_copy(final_send, final_all.at[me], in_sem.at[2])
    own_copy.start()
    steps = sorted(
        itertools.product(range(4), range(2), range(2), range(4), range(2)),
        key=lambda s: -(min(s[0], 4 - s[0]) + s[1] + 2 * s[2] + min(s[3], 4 - s[3])),
    )
    steps.remove((0, 0, 0, 0, 0))
    lasts = []
    for a, b, d, e, f in steps:
        peer = (
            row_of((z + a) % 4, (ylo + b) % 2),
            col_of((yhi + d) % 2, (x + e) % 4, (core + f) % 2),
        )
        copy = pltpu.make_async_remote_copy(
            src_ref=final_send,
            dst_ref=final_all.at[me],
            send_sem=all_sem.at[0],
            recv_sem=all_sem.at[1],
            device_id=peer,
            device_id_type=MESH,
        )
        copy.start()
        lasts.append(peer)
    phase("early2")
    for peer in col_back:
        arrived(early_two.at[peer[0]], two_sem.at[peer[0]], peer)
    total = early_two[0]
    for i in range(1, early_two.shape[0]):
        total = total + early_two[i]
    early_out[...] = total

    phase("waitfinal")
    own_copy.wait()
    others = final_all.at[0 : len(steps)]
    waiter = pltpu.make_async_remote_copy(
        src_ref=others,
        dst_ref=others,
        send_sem=all_sem.at[0],
        recv_sem=all_sem.at[1],
        device_id=lasts[0],
        device_id_type=MESH,
    )
    waiter.wait_recv()
    phase("sum")
    final_out[...] = jnp.sum(final_all[...], axis=0)
    phase("waitsends")
    for copy in sends:
        copy.wait_send()
    waiter.wait_send()
    phase(None)


def finish(scale, shifted, early, final, now, prev, coupling, next_out, alpha_out, beta_out):
    open_scope = []

    def phase(name):
        if open_scope:
            open_scope.pop().__exit__(None, None, None)
        if name:
            open_scope.append(jax.named_scope(name))
            open_scope[0].__enter__()

    phase("Bgram")
    line, lane = iota((8, 16), 0), iota((8, 16), 1)
    flat = jnp.concatenate([final[0:1, :], final[1:2, :]], axis=1) * scale
    flat = jnp.where((iota((8, 256), 1) // 8) % 8 == iota((8, 256), 0), flat, 0.0)
    parts = three_parts(flat)
    place, at = iota((16, 256), 0), iota((16, 256), 1)

    def gathered(block):
        pick = ((at // 64 == block) & (at % 8 == place % 8)).astype(F32).astype(BF16)
        out = lax.dot_general(parts, pick, NT_DIMS, preferred_element_type=F32)
        return (out[0:8] + out[8:16]) + out[16:24]

    cross = gathered(1 + place // 8)
    square = gathered(jnp.where(place < 8, 0, -1))
    known = early[:, 0:16] * scale
    eye = (line == lane).astype(F32)
    shift_eye = (line + 8 == lane).astype(F32)
    coupled = dot_exact(coupling[...], shift_eye, NN_DIMS)
    alpha_t = cross + SHIFT * known[0:8]
    weights = jnp.where(lane < 8, SHIFT * eye - alpha_t, -coupled)
    zeros = jnp.zeros((8, 16), F32)
    mixed = cross + 0.5 * dot_exact(weights, known, NN_DIMS)
    once = dot_exact(mixed, jnp.concatenate([weights, zeros], axis=0), NT_DIMS)
    again = dot_exact(weights, jnp.concatenate([mixed, zeros], axis=0), NT_DIMS)
    residual = shifted[...] + dot_exact(
        weights, jnp.concatenate([now[...], prev[...]], axis=0), NN_DIMS
    )
    phase("Bchol")
    gram = square + (once + again)

    def entry(a, b):
        return jnp.broadcast_to(gram[a : a + 1, b : b + 1], (8, 128))

    upper = {(a, b): entry(a, b) for a in range(8) for b in range(a, 8)}
    inverse = {}
    for a in range(8):
        pivot = 1.0 / upper[a, a]
        for b in range(a + 1, 8):
            factor = upper[a, b] * pivot
            for k in range(b, 8):
                upper[b, k] = upper[b, k] - factor * upper[a, k]
            for k in range(a):
                inverse[b, k] = inverse[b, k] - factor * inverse[a, k]
            inverse[b, a] = -factor
    line, lane = iota((8, 128), 0), iota((8, 128), 1)
    solve = jnp.zeros((8, 128), F32)
    beta = jnp.zeros((8, 128), F32)
    for a in range(8):
        root = jnp.sqrt(upper[a, a])
        scale_row = 1.0 / root
        solve = jnp.where((line == a) & (lane == a), scale_row, solve)
        beta = jnp.where((line == a) & (lane == a), root, beta)
        for k in range(a):
            solve = jnp.where((line == a) & (lane == k), inverse[a, k] * scale_row, solve)
        for b in range(a + 1, 8):
            beta = jnp.where((line == a) & (lane == b), upper[a, b] * scale_row, beta)
    phase("Bsolve")
    next_out[...] = dot_exact(solve[:, 0:8], residual, NN_DIMS)
    beta_out[...] = beta[:, 0:8]
    alpha_out[...] = dot_exact(eye[:, 0:8], alpha_t[:, 0:8], NT_DIMS)
    phase(None)


def local(tiles, tile_rows, tile_cols, tile_counts, block_now, block_prev, coupling, diag_energy):
    slots, tile_width = tiles.shape[2], tiles.shape[3]
    vectors, width = block_now.shape
    n_row, n_col = lax.axis_size("row"), lax.axis_size("col")
    count = width // tile_width
    rows, cols = tile_rows.reshape(1, slots), tile_cols.reshape(1, slots)
    hbm = pl.BlockSpec(memory_space=pltpu.HBM)
    vmem = pl.BlockSpec(memory_space=pltpu.VMEM)
    dma = pltpu.SemaphoreType.DMA
    n_rt, n_ct = n_col * count, n_row * count
    shape = jax.ShapeDtypeStruct
    shifted, early, final = pl.pallas_call(
        kernel,
        out_shape=(shape((vectors, width), F32), shape((16, 128), F32), shape((2, 128), F32)),
        in_specs=[hbm] * 9,
        out_specs=(vmem, vmem, vmem),
        scratch_shapes=[
            pltpu.VMEM((slots, tile_width, tile_width), F32),
            pltpu.VMEM((slots, tile_width, tile_width), BF16),
            pltpu.VMEM((slots, tile_width, tile_width), BF16),
            pltpu.SMEM((slots,), jnp.int32),
            pltpu.SMEM((slots,), jnp.int32),
            pltpu.SMEM((1, 1), jnp.int32),
            pltpu.VMEM((1, slots), jnp.int32),
            pltpu.VMEM((1, slots), jnp.int32),
            pltpu.VMEM((2 * vectors, width), F32),
            pltpu.VMEM((count, tile_width), F32),
            pltpu.VMEM((vectors, n_row * width), F32),
            pltpu.VMEM((vectors, n_col * width), F32),
            pltpu.VMEM((n_ct, 16, tile_width), BF16),
            pltpu.VMEM((n_rt, 16, tile_width), BF16),
            pltpu.VMEM((vectors * slots, tile_width), F32),
            pltpu.VMEM((vectors, n_rt, tile_width), F32),
            pltpu.VMEM((vectors, n_ct, tile_width), F32),
            pltpu.VMEM((vectors, n_rt // 2, tile_width), F32),
            pltpu.VMEM((2, vectors, 2 * count, tile_width), F32),
            pltpu.VMEM((2, vectors, count, tile_width), F32),
            pltpu.VMEM((vectors, count, tile_width), F32),
            pltpu.VMEM((vectors, count, tile_width), F32),
            pltpu.VMEM((2, vectors, 2 * count, tile_width), F32),
            pltpu.VMEM((2, vectors, count, tile_width), F32),
            pltpu.VMEM((vectors, count, tile_width), F32),
            pltpu.VMEM((vectors, count, tile_width), F32),
            pltpu.VMEM((vectors * count, tile_width), F32),
            pltpu.VMEM((2, 16, 128), F32),
            pltpu.VMEM((n_col, 16, 128), F32),
            pltpu.VMEM((n_row, 16, 128), F32),
            pltpu.VMEM((2, 128), F32),
            pltpu.VMEM((n_row * n_col, 2, 128), F32),
            pltpu.VMEM((2, 16, width), BF16),
            dma((slots // CHUNK,)),
            dma((8,)),
            dma((64,)),
            dma((n_row,)),
            dma((n_col,)),
            dma((1,)),
            dma((4,)),
            dma((2,)),
            dma((4,)),
            dma((n_col,)),
            dma((n_row,)),
            dma((2,)),
        ],
        compiler_params=pltpu.CompilerParams(
            collective_id=0, has_side_effects=True, vmem_limit_bytes=52 * 2**20
        ),
    )(
        *(
            value if value is tile_counts else pltpu.with_memory_space_constraint(value, pltpu.HBM)
            for value in (
                tiles.reshape(slots, tile_width, tile_width),
                rows.reshape(slots),
                cols.reshape(slots),
                tile_counts,
                rows,
                cols,
                block_now,
                block_prev,
                diag_energy.reshape(count, tile_width),
            )
        )
    )
    return pl.pallas_call(
        functools.partial(finish, 1.0 / (width * n_row * n_col)),
        out_shape=(shape((vectors, width), F32), shape((8, 8), F32), shape((8, 8), F32)),
        in_specs=[vmem] * 6,
        out_specs=(vmem, vmem, vmem),
        compiler_params=pltpu.CompilerParams(vmem_limit_bytes=4 * 2**20),
    )(shifted, early, final, block_now, block_prev, coupling)


def solution(mesh):
    return jax.shard_map(
        local,
        mesh=mesh,
        in_specs=(
            P("row", "col", None, None, None),
            P("row", "col", None),
            P("row", "col", None),
            P("row", "col"),
            P(None, ("row", "col")),
            P(None, ("row", "col")),
            P(),
            P(("row", "col")),
        ),
        out_specs=(P(None, ("row", "col")), P(), P()),
        check_vma=False,
    )
```

```python
import functools
import itertools

import jax
import jax.numpy as jnp
from jax import lax
from jax.experimental import pallas as pl
from jax.experimental.pallas import tpu as pltpu
from jax.sharding import PartitionSpec as P

MESH = pl.DeviceIdType.MESH
NT_DIMS = (((1,), (1,)), ((), ()))
NN_DIMS = (((1,), (0,)), ((), ()))
F32 = jnp.float32
BF16 = jnp.bfloat16
HIGHEST = lax.Precision.HIGHEST
CHUNK = 16
UNROLL = 64
SHIFT = 2.5


def dot_exact(left, right, dims):
    return lax.dot_general(left, right, dims, precision=HIGHEST, preferred_element_type=F32)


def split_rows(value):
    high = value.astype(BF16).astype(F32)
    return jnp.concatenate([high, value - high], axis=0).astype(BF16)


def three_parts(value):
    high = value.astype(BF16).astype(F32)
    mid = (value - high).astype(BF16).astype(F32)
    return jnp.concatenate([high, mid, (value - high) - mid], axis=0).astype(BF16)


def iota(shape, axis):
    return lax.broadcasted_iota(jnp.int32, shape, axis)


def kernel(
    tiles,
    rows_h,
    cols_h,
    count_h,
    rows_w,
    cols_w,
    now_h,
    prev_h,
    diag_h,
    shifted,
    early_out,
    final_out,
    tile_f32,
    tile_hi,
    tile_lo,
    rows_s,
    cols_s,
    count_s,
    rows_v,
    cols_v,
    lanczos,
    diag,
    col_vec,
    row_vec,
    col_split,
    row_split,
    images,
    part_rows,
    part_cols,
    row_pair,
    row_near,
    row_far,
    row_send,
    row_last,
    col_near,
    col_far,
    col_send,
    col_last,
    image,
    early_send,
    early_one,
    early_two,
    final_send,
    final_all,
    known_split,
    tile_sem,
    in_sem,
    send_sem,
    col_sem,
    row_sem,
    pair_sem,
    ring_sem,
    last_sem,
    back_sem,
    one_sem,
    two_sem,
    all_sem,
):
    r = lax.axis_index("row")
    c = lax.axis_index("col")
    z, ylo = r // 2, r % 2
    yhi, x, core = c // 8, (c // 2) % 4, c % 2
    slots = tiles.shape[0]
    width = now_h.shape[1]
    count = width // 128
    open_scope = []

    def phase(name):
        if open_scope:
            open_scope.pop().__exit__(None, None, None)
        if name:
            open_scope.append(jax.named_scope(name))
            open_scope[0].__enter__()

    def row_of(zz, yy):
        return zz * 2 + yy

    def col_of(yy, xx, cc):
        return yy * 8 + xx * 2 + cc

    zs = [(z + d) % 4 for d in (2, 1, 3)]
    xs = [(x + d) % 4 for d in (2, 1, 3)]
    row_peer = row_of(z, 1 - ylo)
    col_peer = col_of(1 - yhi, x, core)
    pair = col_of(yhi, x, 1 - core)
    zn, xn = zs[1:], xs[1:]
    across = (r, col_of(1 - yhi, xs[0], core))
    far = (row_of(zs[0], 1 - ylo), c)
    col_steps = [(2, 1), (1, 1), (3, 1), (2, 0), (0, 1), (1, 0), (3, 0)]
    col_group = [(row_of((z + a) % 4, (ylo + b) % 2), c) for a, b in col_steps]
    col_back = [(row_of((z + 4 - a) % 4, (ylo + b) % 2), c) for a, b in col_steps]

    phase("start")
    barrier = pltpu.get_barrier_semaphore()
    first_peers = [(row_peer, c), (r, col_peer), far] + [(row_of(zz, ylo), c) for zz in zs]
    first_peers += [(r, col_of(yhi, xx, core)) for xx in xs] + [(r, pair)]
    for peer in first_peers:
        pl.semaphore_signal(barrier, inc=1, device_id=peer, device_id_type=MESH)

    now, prev = lanczos.at[0:8], lanczos.at[8:16]
    loads = [
        pltpu.make_async_copy(src, dst, in_sem.at[i])
        for i, (src, dst) in enumerate(
            [
                (now_h, now),
                (prev_h, prev),
                (diag_h, diag),
                (rows_h, rows_s),
                (cols_h, cols_s),
                (count_h, count_s),
                (rows_w, rows_v),
                (cols_w, cols_v),
            ]
        )
    ]
    loads[0].start()
    chunks = slots // CHUNK

    def tile_copy(i):
        part = pl.ds(i * CHUNK, CHUNK)
        return pltpu.make_async_copy(tiles.at[part], tile_f32.at[part], tile_sem.at[i])

    def piece(ref, p):
        return ref.at[:, pl.ds(pl.multiple_of(p * width, width), width)]

    loads[0].wait()
    for i in range(chunks):
        tile_copy(i).start()
    for copy in loads[1:]:
        copy.start()
    phase("barrier")
    pl.semaphore_wait(barrier, len(first_peers))

    sends = []
    numbers = itertools.count()

    def send(src, dst, recv, peer):
        copy = pltpu.make_async_remote_copy(
            src_ref=src,
            dst_ref=dst,
            send_sem=send_sem.at[next(numbers)],
            recv_sem=recv,
            device_id=peer,
            device_id_type=MESH,
        )
        copy.start()
        sends.append(copy)

    def arrived(dst, recv, peer):
        pltpu.make_async_remote_copy(
            src_ref=dst,
            dst_ref=dst,
            send_sem=send_sem.at[0],
            recv_sem=recv,
            device_id=peer,
            device_id_type=MESH,
        ).wait_recv()

    phase("send1")
    send(now, piece(col_vec, r), col_sem.at[r], (row_peer, c))
    send(now, piece(row_vec, c), row_sem.at[c], (r, col_peer))
    send(now, piece(col_vec, r), col_sem.at[r], far)
    for zz in zs:
        send(now, piece(col_vec, r), col_sem.at[r], (row_of(zz, ylo), c))
    for xx in xs:
        send(now, piece(row_vec, c), row_sem.at[c], (r, col_of(yhi, xx, core)))
    send(now, piece(row_vec, c), row_sem.at[c], (r, pair))
    piece(col_vec, r)[...] = now[...]
    piece(row_vec, c)[...] = now[...]

    def convert(first, last):
        def chunk(i, _):
            tile_copy(i).wait()

            def one(j, _):
                value = tile_f32[i * CHUNK + j]
                high = value.astype(BF16)
                tile_hi[i * CHUNK + j] = high
                tile_lo[i * CHUNK + j] = (value - high.astype(F32)).astype(BF16)
                return 0

            lax.fori_loop(0, CHUNK, one, 0, unroll=8)
            return 0

        lax.fori_loop(first, last, chunk, 0)

    phase("conv1")
    convert(0, 9)
    phase("fwdrow")
    arrived(piece(col_vec, row_peer), col_sem.at[row_peer], (row_peer, c))
    for zz in zn:
        send(
            piece(col_vec, row_peer), piece(col_vec, row_peer), col_sem.at[row_peer], (row_of(zz, ylo), c)
        )
    phase("fwdcol")
    arrived(piece(row_vec, col_peer), row_sem.at[col_peer], (r, col_peer))
    for xx in xs:
        send(
            piece(row_vec, col_peer),
            piece(row_vec, col_peer),
            row_sem.at[col_peer],
            (r, col_of(yhi, xx, core)),
        )
    send(piece(row_vec, col_peer), piece(row_vec, col_peer), row_sem.at[col_peer], (r, pair))
    phase("conv2")
    convert(9, chunks)
    for copy in loads[1:]:
        copy.wait()
    phase("early")
    early_send[...] = jnp.zeros_like(early_send)
    known = lanczos[...]
    high = known.astype(BF16)
    known_split[0] = high
    known_split[1] = (known - high.astype(F32)).astype(BF16)
    early_send[0, :, 0:16] = dot_exact(known, known, NT_DIMS)

    phase("waitcolvec")
    for zz in zn:
        for yy in (ylo, 1 - ylo):
            p = row_of(zz, yy)
            arrived(piece(col_vec, p), col_sem.at[p], (row_of(zz, ylo), c))
    for p in (row_of(zs[0], ylo), far[0]):
        arrived(piece(col_vec, p), col_sem.at[p], (p, c))

    def split_vectors(src, dst):
        def one(t, _):
            dst[t] = split_rows(src[:, pl.ds(pl.multiple_of(t * 128, 128), 128)])
            return 0

        lax.fori_loop(0, dst.shape[0], one, 0, unroll=16)

    phase("split1")
    split_vectors(col_vec, col_split)

    def products(first, last, index, vectors, transposed):
        for m in range(first, last):
            left = vectors[index[m]]
            if transposed:
                weights = jnp.concatenate([tile_hi[m], tile_lo[m]], axis=0)
                out = lax.dot_general(left, weights, NT_DIMS, preferred_element_type=F32)
            else:
                weights = jnp.concatenate([tile_hi[m], tile_lo[m]], axis=1)
                out = lax.dot_general(left, weights, NN_DIMS, preferred_element_type=F32)
            total = (out[0:8, 0:128] + out[8:16, 0:128]) + out[0:8, 128:256]
            images[pl.ds(m, 8, stride=slots), :] = total

    used = iota((1, slots), 1) < count_s[0, 0]

    def scatter(place, dst):
        wanted = jnp.where(used, place, -1)
        pick = (iota((dst.shape[1], slots), 0) == wanted).astype(F32).astype(BF16)
        for v in range(8):
            value = images[v * slots : (v + 1) * slots, :]
            high = value.astype(BF16)
            low = (value - high.astype(F32)).astype(BF16)
            out = lax.dot_general(
                pick, jnp.concatenate([high, low], axis=1), NN_DIMS, preferred_element_type=F32
            )
            dst[v] = out[:, 0:128] + out[:, 128:256]

    phase("prodrows1")
    products(0, 2 * UNROLL, cols_s, col_split, True)
    phase("relay")
    for yy in (yhi, 1 - yhi):
        for xx in xs:
            p = col_of(yy, xx, core)
            arrived(piece(row_vec, p), row_sem.at[p], (r, col_of(yhi, xx, core)))
            send(piece(row_vec, p), piece(row_vec, p), row_sem.at[p], (r, pair))
    phase("prodrows2")
    products(2 * UNROLL, slots, cols_s, col_split, True)
    phase("scatrows")
    place = rows_v[...]
    owner = place // 16
    scatter(
        ((owner % 2) * 8 + ((owner // 2) % 4) * 2 + owner // 8) * 16 + place % 16, part_rows
    )
    half = part_rows.shape[1] // 2

    def half_of(cc):
        return part_rows.at[:, pl.ds(pl.multiple_of(cc * half, half), half), :]

    send(half_of(1 - core), row_pair, pair_sem.at[0], (r, pair))

    phase("waitrowvec")
    for yy in (yhi, 1 - yhi):
        for xx in [x] + xs:
            p = col_of(yy, xx, 1 - core)
            arrived(piece(row_vec, p), row_sem.at[p], (r, pair))
    row_steps = list(itertools.product(range(2), range(4), range(2)))[1:]
    row_group = [(r, col_of((yhi + a) % 2, (x + b) % 4, (core + d) % 2)) for a, b, d in row_steps]
    row_back = [
        (r, col_of((yhi + a) % 2, (x + 4 - b) % 4, (core + d) % 2)) for a, b, d in row_steps
    ]
    phase("split2")
    split_vectors(row_vec, row_split)
    phase("prodcols1")
    products(0, UNROLL, rows_s, row_split, False)
    phase("waitpair")
    arrived(row_pair, pair_sem.at[0], (r, pair))
    mine = half_of(core)
    for v in range(8):
        row_pair[v] = row_pair[v] + mine[v]
    for d, xx in enumerate(xn):
        send(
            row_pair.at[:, pl.ds(pl.multiple_of(xx * 2 * count, 2 * count), 2 * count), :],
            row_near.at[d],
            ring_sem.at[d],
            (r, col_of(yhi, xx, core)),
        )
    early_one[c] = early_send[0]
    for peer in row_group:
        send(early_send.at[0], early_one.at[c], one_sem.at[c], peer)
    phase("prodcols2")
    products(UNROLL, 3 * UNROLL, rows_s, row_split, False)
    phase("rowfar")
    opposite = xs[0] * 2 * count
    for d, (yy, peer) in enumerate([(1 - yhi, across), (yhi, (r, col_of(yhi, xs[0], core)))]):
        send(
            row_pair.at[:, pl.ds(pl.multiple_of(opposite + yy * count, count), count), :],
            row_far.at[d],
            ring_sem.at[2 + d],
            peer,
        )
    phase("prodcols3")
    products(3 * UNROLL, slots, rows_s, row_split, False)
    phase("scatcols")
    scatter(cols_v[...], part_cols)

    def lot(ref, k):
        return ref.at[:, pl.ds(pl.multiple_of(k * count, count), count), :]

    for d, zz in enumerate(zn):
        send(
            part_cols.at[:, pl.ds(pl.multiple_of(zz * 2 * count, 2 * count), 2 * count), :],
            col_near.at[d],
            back_sem.at[d],
            (row_of(zz, ylo), c),
        )
    send(lot(part_cols, far[0]), col_far.at[0], back_sem.at[2], far)
    phase("rownear")
    for d in range(2):
        arrived(row_near.at[d], ring_sem.at[d], (r, col_of(yhi, xn[1 - d], core)))
    mine_at = pl.multiple_of(x * 2 * count + yhi * count, count)
    away_at = pl.multiple_of(x * 2 * count + (1 - yhi) * count, count)
    for v in range(8):
        at = pl.ds(pl.multiple_of((1 - yhi) * count, count), count)
        row_send[v] = row_pair[v, pl.ds(away_at, count), :] + (row_near[0, v, at, :] + row_near[1, v, at, :])
    send(row_send, row_last, last_sem.at[0], (r, col_peer))
    phase("colfar")
    send(
        lot(part_cols, row_of(zs[0], ylo)), col_far.at[1], back_sem.at[3], (row_of(zs[0], ylo), c)
    )
    phase("near")
    for d in range(2):
        arrived(col_near.at[d], back_sem.at[d], (row_of(zn[1 - d], ylo), c))
    at = pl.multiple_of((1 - ylo) * count, count)
    away = lot(part_cols, row_peer)
    for v in range(8):
        col_send[v] = away[v] + (col_near[0, v, pl.ds(at, count), :] + col_near[1, v, pl.ds(at, count), :])
    send(col_send, col_last, last_sem.at[1], (row_peer, c))

    phase("waitfar")
    arrived(row_far.at[0], ring_sem.at[2], across)
    arrived(row_far.at[1], ring_sem.at[3], (r, col_of(yhi, xs[0], core)))
    arrived(col_far.at[0], back_sem.at[2], far)
    arrived(col_far.at[1], back_sem.at[3], (row_of(zs[0], ylo), c))
    home = pl.ds(pl.multiple_of(ylo * count, count), count)
    own = pl.ds(pl.multiple_of(yhi * count, count), count)
    col_mine = lot(part_cols, r)
    for v in range(8):
        total = (row_pair[v, pl.ds(mine_at, count), :] + col_mine[v]) + (col_far[0, v] + col_far[1, v])
        total = total + (row_far[0, v] + row_far[1, v])
        total = total + (row_near[0, v, own, :] + row_near[1, v, own, :])
        image[v * count : (v + 1) * count, :] = total + (col_near[0, v, home, :] + col_near[1, v, home, :])
    phase("early1")
    for peer in row_back:
        arrived(early_one.at[peer[1]], one_sem.at[peer[1]], peer)
    total = early_one[0]
    for i in range(1, early_one.shape[0]):
        total = total + early_one[i]
    early_send[1] = total
    early_two[r] = total
    for peer in col_group:
        send(early_send.at[1], early_two.at[r], two_sem.at[r], peer)
    phase("waitlast")
    arrived(col_last, last_sem.at[1], (row_peer, c))
    arrived(row_last, last_sem.at[0], (r, col_peer))
    phase("shifted")
    for v in range(8):
        part = slice(v * count, (v + 1) * count)
        image[part, :] = image[part, :] + (row_last[v] + col_last[v])
    for t in range(count):
        at = slice(t * 128, (t + 1) * 128)
        shifted[:, at] = image[pl.ds(t, 8, stride=count), :] + (diag[t : t + 1, :] - SHIFT) * now[:, at]

    phase("gram")
    halves = split_rows(shifted[...])
    gram = lax.dot_general(
        halves,
        jnp.concatenate([halves, known_split[0], known_split[1]], axis=0),
        NT_DIMS,
        preferred_element_type=F32,
    )
    gram = gram[0:8] + gram[8:16]
    place, lane = iota((48, 256), 0), iota((48, 256), 1)
    block = jnp.where(place < 16, 0, 1 + (place // 8) % 2)
    spread = ((lane // 64 == block) & (lane % 8 == place % 8)).astype(F32).astype(BF16)
    flat = lax.dot_general(three_parts(gram), spread, NN_DIMS, preferred_element_type=F32)
    flat = (flat[0:8] + flat[8:16]) + flat[16:24]
    flat = jnp.where((iota((8, 256), 1) // 8) % 8 == iota((8, 256), 0), flat, 0.0)
    flat = jnp.sum(flat, axis=0, keepdims=True)
    final_send[0:1, :] = flat[:, 0:128]
    final_send[1:2, :] = flat[:, 128:256]
    phase("final")
    me = r * early_one.shape[0] + c
    own_copy = pltpu.make_async_copy(final_send, final_all.at[me], in_sem.at[2])
    own_copy.start()
    steps = sorted(
        itertools.product(range(4), range(2), range(2), range(4), range(2)),
        key=lambda s: -(min(s[0], 4 - s[0]) + s[1] + 2 * s[2] + min(s[3], 4 - s[3])),
    )
    steps.remove((0, 0, 0, 0, 0))
    lasts = []
    for a, b, d, e, f in steps:
        peer = (
            row_of((z + a) % 4, (ylo + b) % 2),
            col_of((yhi + d) % 2, (x + e) % 4, (core + f) % 2),
        )
        copy = pltpu.make_async_remote_copy(
            src_ref=final_send,
            dst_ref=final_all.at[me],
            send_sem=all_sem.at[0],
            recv_sem=all_sem.at[1],
            device_id=peer,
            device_id_type=MESH,
        )
        copy.start()
        lasts.append(peer)
    phase("early2")
    for peer in col_back:
        arrived(early_two.at[peer[0]], two_sem.at[peer[0]], peer)
    total = early_two[0]
    for i in range(1, early_two.shape[0]):
        total = total + early_two[i]
    early_out[...] = total

    phase("waitfinal")
    own_copy.wait()
    others = final_all.at[0 : len(steps)]
    waiter = pltpu.make_async_remote_copy(
        src_ref=others,
        dst_ref=others,
        send_sem=all_sem.at[0],
        recv_sem=all_sem.at[1],
        device_id=lasts[0],
        device_id_type=MESH,
    )
    waiter.wait_recv()
    phase("sum")
    final_out[...] = jnp.sum(final_all[...], axis=0)
    phase("waitsends")
    for copy in sends:
        copy.wait_send()
    waiter.wait_send()
    phase(None)


def finish(scale, shifted, early, final, now, prev, coupling, next_out, alpha_out, beta_out):
    open_scope = []

    def phase(name):
        if open_scope:
            open_scope.pop().__exit__(None, None, None)
        if name:
            open_scope.append(jax.named_scope(name))
            open_scope[0].__enter__()

    phase("Bgram")
    line, lane = iota((8, 16), 0), iota((8, 16), 1)
    flat = jnp.concatenate([final[0:1, :], final[1:2, :]], axis=1) * scale
    flat = jnp.where((iota((8, 256), 1) // 8) % 8 == iota((8, 256), 0), flat, 0.0)
    parts = three_parts(flat)
    place, at = iota((16, 256), 0), iota((16, 256), 1)

    def gathered(block):
        pick = ((at // 64 == block) & (at % 8 == place % 8)).astype(F32).astype(BF16)
        out = lax.dot_general(parts, pick, NT_DIMS, preferred_element_type=F32)
        return (out[0:8] + out[8:16]) + out[16:24]

    cross = gathered(1 + place // 8)
    square = gathered(jnp.where(place < 8, 0, -1))
    known = early[:, 0:16] * scale
    eye = (line == lane).astype(F32)
    shift_eye = (line + 8 == lane).astype(F32)
    coupled = dot_exact(coupling[...], shift_eye, NN_DIMS)
    alpha_t = cross + SHIFT * known[0:8]
    weights = jnp.where(lane < 8, SHIFT * eye - alpha_t, -coupled)
    zeros = jnp.zeros((8, 16), F32)
    mixed = cross + 0.5 * dot_exact(weights, known, NN_DIMS)
    once = dot_exact(mixed, jnp.concatenate([weights, zeros], axis=0), NT_DIMS)
    again = dot_exact(weights, jnp.concatenate([mixed, zeros], axis=0), NT_DIMS)
    residual = shifted[...] + dot_exact(
        weights, jnp.concatenate([now[...], prev[...]], axis=0), NN_DIMS
    )
    phase("Bchol")
    gram = square + (once + again)

    def entry(a, b):
        return jnp.broadcast_to(gram[a : a + 1, b : b + 1], (8, 128))

    upper = {(a, b): entry(a, b) for a in range(8) for b in range(a, 8)}
    inverse = {}
    for a in range(8):
        pivot = 1.0 / upper[a, a]
        for b in range(a + 1, 8):
            factor = upper[a, b] * pivot
            for k in range(b, 8):
                upper[b, k] = upper[b, k] - factor * upper[a, k]
            for k in range(a):
                inverse[b, k] = inverse[b, k] - factor * inverse[a, k]
            inverse[b, a] = -factor
    line, lane = iota((8, 128), 0), iota((8, 128), 1)
    solve = jnp.zeros((8, 128), F32)
    beta = jnp.zeros((8, 128), F32)
    for a in range(8):
        root = jnp.sqrt(upper[a, a])
        scale_row = 1.0 / root
        solve = jnp.where((line == a) & (lane == a), scale_row, solve)
        beta = jnp.where((line == a) & (lane == a), root, beta)
        for k in range(a):
            solve = jnp.where((line == a) & (lane == k), inverse[a, k] * scale_row, solve)
        for b in range(a + 1, 8):
            beta = jnp.where((line == a) & (lane == b), upper[a, b] * scale_row, beta)
    phase("Bsolve")
    next_out[...] = dot_exact(solve[:, 0:8], residual, NN_DIMS)
    beta_out[...] = beta[:, 0:8]
    alpha_out[...] = dot_exact(eye[:, 0:8], alpha_t[:, 0:8], NT_DIMS)
    phase(None)


def local(tiles, tile_rows, tile_cols, tile_counts, block_now, block_prev, coupling, diag_energy):
    slots, tile_width = tiles.shape[2], tiles.shape[3]
    vectors, width = block_now.shape
    n_row, n_col = lax.axis_size("row"), lax.axis_size("col")
    count = width // tile_width
    rows, cols = tile_rows.reshape(1, slots), tile_cols.reshape(1, slots)
    hbm = pl.BlockSpec(memory_space=pltpu.HBM)
    vmem = pl.BlockSpec(memory_space=pltpu.VMEM)
    dma = pltpu.SemaphoreType.DMA
    n_rt, n_ct = n_col * count, n_row * count
    shape = jax.ShapeDtypeStruct
    shifted, early, final = pl.pallas_call(
        kernel,
        out_shape=(shape((vectors, width), F32), shape((16, 128), F32), shape((2, 128), F32)),
        in_specs=[hbm] * 9,
        out_specs=(vmem, vmem, vmem),
        scratch_shapes=[
            pltpu.VMEM((slots, tile_width, tile_width), F32),
            pltpu.VMEM((slots, tile_width, tile_width), BF16),
            pltpu.VMEM((slots, tile_width, tile_width), BF16),
            pltpu.SMEM((slots,), jnp.int32),
            pltpu.SMEM((slots,), jnp.int32),
            pltpu.SMEM((1, 1), jnp.int32),
            pltpu.VMEM((1, slots), jnp.int32),
            pltpu.VMEM((1, slots), jnp.int32),
            pltpu.VMEM((2 * vectors, width), F32),
            pltpu.VMEM((count, tile_width), F32),
            pltpu.VMEM((vectors, n_row * width), F32),
            pltpu.VMEM((vectors, n_col * width), F32),
            pltpu.VMEM((n_ct, 16, tile_width), BF16),
            pltpu.VMEM((n_rt, 16, tile_width), BF16),
            pltpu.VMEM((vectors * slots, tile_width), F32),
            pltpu.VMEM((vectors, n_rt, tile_width), F32),
            pltpu.VMEM((vectors, n_ct, tile_width), F32),
            pltpu.VMEM((vectors, n_rt // 2, tile_width), F32),
            pltpu.VMEM((2, vectors, 2 * count, tile_width), F32),
            pltpu.VMEM((2, vectors, count, tile_width), F32),
            pltpu.VMEM((vectors, count, tile_width), F32),
            pltpu.VMEM((vectors, count, tile_width), F32),
            pltpu.VMEM((2, vectors, 2 * count, tile_width), F32),
            pltpu.VMEM((2, vectors, count, tile_width), F32),
            pltpu.VMEM((vectors, count, tile_width), F32),
            pltpu.VMEM((vectors, count, tile_width), F32),
            pltpu.VMEM((vectors * count, tile_width), F32),
            pltpu.VMEM((2, 16, 128), F32),
            pltpu.VMEM((n_col, 16, 128), F32),
            pltpu.VMEM((n_row, 16, 128), F32),
            pltpu.VMEM((2, 128), F32),
            pltpu.VMEM((n_row * n_col, 2, 128), F32),
            pltpu.VMEM((2, 16, width), BF16),
            dma((slots // CHUNK,)),
            dma((8,)),
            dma((64,)),
            dma((n_row,)),
            dma((n_col,)),
            dma((1,)),
            dma((4,)),
            dma((2,)),
            dma((4,)),
            dma((n_col,)),
            dma((n_row,)),
            dma((2,)),
        ],
        compiler_params=pltpu.CompilerParams(
            collective_id=0, has_side_effects=True, vmem_limit_bytes=52 * 2**20
        ),
    )(
        *(
            value if value is tile_counts else pltpu.with_memory_space_constraint(value, pltpu.HBM)
            for value in (
                tiles.reshape(slots, tile_width, tile_width),
                rows.reshape(slots),
                cols.reshape(slots),
                tile_counts,
                rows,
                cols,
                block_now,
                block_prev,
                diag_energy.reshape(count, tile_width),
            )
        )
    )
    return pl.pallas_call(
        functools.partial(finish, 1.0 / (width * n_row * n_col)),
        out_shape=(shape((vectors, width), F32), shape((8, 8), F32), shape((8, 8), F32)),
        in_specs=[vmem] * 6,
        out_specs=(vmem, vmem, vmem),
        compiler_params=pltpu.CompilerParams(vmem_limit_bytes=4 * 2**20),
    )(shifted, early, final, block_now, block_prev, coupling)


def solution(mesh):
    return jax.shard_map(
        local,
        mesh=mesh,
        in_specs=(
            P("row", "col", None, None, None),
            P("row", "col", None),
            P("row", "col", None),
            P("row", "col"),
            P(None, ("row", "col")),
            P(None, ("row", "col")),
            P(),
            P(("row", "col")),
        ),
        out_specs=(P(None, ("row", "col")), P(), P()),
        check_vma=False,
    )
```

```python
import functools
import itertools

import jax
import jax.numpy as jnp
from jax import lax
from jax.experimental import pallas as pl
from jax.experimental.pallas import tpu as pltpu
from jax.sharding import PartitionSpec as P

MESH = pl.DeviceIdType.MESH
NT_DIMS = (((1,), (1,)), ((), ()))
NN_DIMS = (((1,), (0,)), ((), ()))
F32 = jnp.float32
BF16 = jnp.bfloat16
HIGHEST = lax.Precision.HIGHEST
CHUNK = 16
UNROLL = 64
SHIFT = 2.5


def dot_exact(left, right, dims):
    return lax.dot_general(left, right, dims, precision=HIGHEST, preferred_element_type=F32)


def split_rows(value):
    high = value.astype(BF16).astype(F32)
    return jnp.concatenate([high, value - high], axis=0).astype(BF16)


def three_parts(value):
    high = value.astype(BF16).astype(F32)
    mid = (value - high).astype(BF16).astype(F32)
    return jnp.concatenate([high, mid, (value - high) - mid], axis=0).astype(BF16)


def iota(shape, axis):
    return lax.broadcasted_iota(jnp.int32, shape, axis)


def kernel(
    tiles,
    rows_h,
    cols_h,
    count_h,
    rows_w,
    cols_w,
    now_h,
    prev_h,
    diag_h,
    shifted,
    early_out,
    final_out,
    tile_f32,
    tile_hi,
    tile_lo,
    rows_s,
    cols_s,
    count_s,
    rows_v,
    cols_v,
    lanczos,
    diag,
    col_vec,
    row_vec,
    col_split,
    row_split,
    images,
    part_rows,
    part_cols,
    row_pair,
    row_near,
    row_far,
    row_send,
    row_last,
    col_near,
    col_far,
    col_send,
    col_last,
    image,
    early_send,
    early_one,
    early_two,
    final_send,
    final_all,
    known_split,
    tile_sem,
    in_sem,
    send_sem,
    col_sem,
    row_sem,
    pair_sem,
    ring_sem,
    last_sem,
    back_sem,
    one_sem,
    two_sem,
    all_sem,
):
    r = lax.axis_index("row")
    c = lax.axis_index("col")
    z, ylo = r // 2, r % 2
    yhi, x, core = c // 8, (c // 2) % 4, c % 2
    slots = tiles.shape[0]
    width = now_h.shape[1]
    count = width // 128
    open_scope = []

    def phase(name):
        if open_scope:
            open_scope.pop().__exit__(None, None, None)
        if name:
            open_scope.append(jax.named_scope(name))
            open_scope[0].__enter__()

    def row_of(zz, yy):
        return zz * 2 + yy

    def col_of(yy, xx, cc):
        return yy * 8 + xx * 2 + cc

    zs = [(z + d) % 4 for d in (2, 1, 3)]
    xs = [(x + d) % 4 for d in (2, 1, 3)]
    row_peer = row_of(z, 1 - ylo)
    col_peer = col_of(1 - yhi, x, core)
    pair = col_of(yhi, x, 1 - core)
    zn, xn = zs[1:], xs[1:]
    across = (r, col_of(1 - yhi, xs[0], core))
    far = (row_of(zs[0], 1 - ylo), c)
    col_steps = [(2, 1), (1, 1), (3, 1), (2, 0), (0, 1), (1, 0), (3, 0)]
    col_group = [(row_of((z + a) % 4, (ylo + b) % 2), c) for a, b in col_steps]
    col_back = [(row_of((z + 4 - a) % 4, (ylo + b) % 2), c) for a, b in col_steps]

    phase("start")
    barrier = pltpu.get_barrier_semaphore()
    first_peers = [(row_peer, c), (r, col_peer), far] + [(row_of(zz, ylo), c) for zz in zs]
    first_peers += [(r, col_of(yhi, xx, core)) for xx in xs] + [(r, pair)]
    for peer in first_peers:
        pl.semaphore_signal(barrier, inc=1, device_id=peer, device_id_type=MESH)

    now, prev = lanczos.at[0:8], lanczos.at[8:16]
    loads = [
        pltpu.make_async_copy(src, dst, in_sem.at[i])
        for i, (src, dst) in enumerate(
            [
                (now_h, now),
                (prev_h, prev),
                (diag_h, diag),
                (rows_h, rows_s),
                (cols_h, cols_s),
                (count_h, count_s),
                (rows_w, rows_v),
                (cols_w, cols_v),
            ]
        )
    ]
    loads[0].start()
    chunks = slots // CHUNK

    def tile_copy(i):
        part = pl.ds(i * CHUNK, CHUNK)
        return pltpu.make_async_copy(tiles.at[part], tile_f32.at[part], tile_sem.at[i])

    def piece(ref, p):
        return ref.at[:, pl.ds(pl.multiple_of(p * width, width), width)]

    loads[0].wait()
    for i in range(chunks):
        tile_copy(i).start()
    for copy in loads[1:]:
        copy.start()
    phase("barrier")
    pl.semaphore_wait(barrier, len(first_peers))

    sends = []
    numbers = itertools.count()

    def send(src, dst, recv, peer):
        copy = pltpu.make_async_remote_copy(
            src_ref=src,
            dst_ref=dst,
            send_sem=send_sem.at[next(numbers)],
            recv_sem=recv,
            device_id=peer,
            device_id_type=MESH,
        )
        copy.start()
        sends.append(copy)

    def arrived(dst, recv, peer):
        pltpu.make_async_remote_copy(
            src_ref=dst,
            dst_ref=dst,
            send_sem=send_sem.at[0],
            recv_sem=recv,
            device_id=peer,
            device_id_type=MESH,
        ).wait_recv()

    phase("send1")
    send(now, piece(col_vec, r), col_sem.at[r], (row_peer, c))
    send(now, piece(row_vec, c), row_sem.at[c], (r, col_peer))
    send(now, piece(col_vec, r), col_sem.at[r], far)
    for zz in zs:
        send(now, piece(col_vec, r), col_sem.at[r], (row_of(zz, ylo), c))
    for xx in xs:
        send(now, piece(row_vec, c), row_sem.at[c], (r, col_of(yhi, xx, core)))
    send(now, piece(row_vec, c), row_sem.at[c], (r, pair))
    piece(col_vec, r)[...] = now[...]
    piece(row_vec, c)[...] = now[...]

    def convert(first, last):
        def chunk(i, _):
            tile_copy(i).wait()

            def one(j, _):
                value = tile_f32[i * CHUNK + j]
                high = value.astype(BF16)
                tile_hi[i * CHUNK + j] = high
                tile_lo[i * CHUNK + j] = (value - high.astype(F32)).astype(BF16)
                return 0

            lax.fori_loop(0, CHUNK, one, 0, unroll=8)
            return 0

        lax.fori_loop(first, last, chunk, 0)

    phase("conv1")
    convert(0, 9)
    phase("fwdrow")
    arrived(piece(col_vec, row_peer), col_sem.at[row_peer], (row_peer, c))
    for zz in zn:
        send(
            piece(col_vec, row_peer), piece(col_vec, row_peer), col_sem.at[row_peer], (row_of(zz, ylo), c)
        )
    phase("fwdcol")
    arrived(piece(row_vec, col_peer), row_sem.at[col_peer], (r, col_peer))
    for xx in xs:
        send(
            piece(row_vec, col_peer),
            piece(row_vec, col_peer),
            row_sem.at[col_peer],
            (r, col_of(yhi, xx, core)),
        )
    send(piece(row_vec, col_peer), piece(row_vec, col_peer), row_sem.at[col_peer], (r, pair))
    phase("conv2")
    convert(9, chunks)
    for copy in loads[1:]:
        copy.wait()
    phase("early")
    early_send[...] = jnp.zeros_like(early_send)
    known = lanczos[...]
    high = known.astype(BF16)
    known_split[0] = high
    known_split[1] = (known - high.astype(F32)).astype(BF16)
    early_send[0, :, 0:16] = dot_exact(known, known, NT_DIMS)

    phase("waitcolvec")
    for zz in zn:
        for yy in (ylo, 1 - ylo):
            p = row_of(zz, yy)
            arrived(piece(col_vec, p), col_sem.at[p], (row_of(zz, ylo), c))
    for p in (row_of(zs[0], ylo), far[0]):
        arrived(piece(col_vec, p), col_sem.at[p], (p, c))

    def split_vectors(src, dst):
        def one(t, _):
            dst[t] = split_rows(src[:, pl.ds(pl.multiple_of(t * 128, 128), 128)])
            return 0

        lax.fori_loop(0, dst.shape[0], one, 0, unroll=16)

    phase("split1")
    split_vectors(col_vec, col_split)

    def products(first, last, index, vectors, transposed):
        for m in range(first, last):
            left = vectors[index[m]]
            if transposed:
                weights = jnp.concatenate([tile_hi[m], tile_lo[m]], axis=0)
                out = lax.dot_general(left, weights, NT_DIMS, preferred_element_type=F32)
            else:
                weights = jnp.concatenate([tile_hi[m], tile_lo[m]], axis=1)
                out = lax.dot_general(left, weights, NN_DIMS, preferred_element_type=F32)
            total = (out[0:8, 0:128] + out[8:16, 0:128]) + out[0:8, 128:256]
            images[pl.ds(m, 8, stride=slots), :] = total

    used = iota((1, slots), 1) < count_s[0, 0]

    def scatter(place, dst):
        wanted = jnp.where(used, place, -1)
        pick = (iota((dst.shape[1], slots), 0) == wanted).astype(F32).astype(BF16)
        for v in range(8):
            value = images[v * slots : (v + 1) * slots, :]
            high = value.astype(BF16)
            low = (value - high.astype(F32)).astype(BF16)
            out = lax.dot_general(
                pick, jnp.concatenate([high, low], axis=1), NN_DIMS, preferred_element_type=F32
            )
            dst[v] = out[:, 0:128] + out[:, 128:256]

    phase("prodrows1")
    products(0, 2 * UNROLL, cols_s, col_split, True)
    phase("relay")
    for yy in (yhi, 1 - yhi):
        for xx in xs:
            p = col_of(yy, xx, core)
            arrived(piece(row_vec, p), row_sem.at[p], (r, col_of(yhi, xx, core)))
            send(piece(row_vec, p), piece(row_vec, p), row_sem.at[p], (r, pair))
    phase("prodrows2")
    products(2 * UNROLL, slots, cols_s, col_split, True)
    phase("scatrows")
    place = rows_v[...]
    owner = place // 16
    scatter(
        ((owner % 2) * 8 + ((owner // 2) % 4) * 2 + owner // 8) * 16 + place % 16, part_rows
    )
    half = part_rows.shape[1] // 2

    def half_of(cc):
        return part_rows.at[:, pl.ds(pl.multiple_of(cc * half, half), half), :]

    send(half_of(1 - core), row_pair, pair_sem.at[0], (r, pair))

    phase("waitrowvec")
    for yy in (yhi, 1 - yhi):
        for xx in [x] + xs:
            p = col_of(yy, xx, 1 - core)
            arrived(piece(row_vec, p), row_sem.at[p], (r, pair))
    row_steps = list(itertools.product(range(2), range(4), range(2)))[1:]
    row_group = [(r, col_of((yhi + a) % 2, (x + b) % 4, (core + d) % 2)) for a, b, d in row_steps]
    row_back = [
        (r, col_of((yhi + a) % 2, (x + 4 - b) % 4, (core + d) % 2)) for a, b, d in row_steps
    ]
    phase("split2")
    split_vectors(row_vec, row_split)
    phase("prodcols1")
    products(0, 2 * UNROLL, rows_s, row_split, False)
    phase("waitpair")
    arrived(row_pair, pair_sem.at[0], (r, pair))
    mine = half_of(core)
    for v in range(8):
        row_pair[v] = row_pair[v] + mine[v]
    for d, xx in enumerate(xn):
        send(
            row_pair.at[:, pl.ds(pl.multiple_of(xx * 2 * count, 2 * count), 2 * count), :],
            row_near.at[d],
            ring_sem.at[d],
            (r, col_of(yhi, xx, core)),
        )
    early_one[c] = early_send[0]
    for peer in row_group:
        send(early_send.at[0], early_one.at[c], one_sem.at[c], peer)
    phase("prodcols2")
    products(2 * UNROLL, 3 * UNROLL, rows_s, row_split, False)
    phase("prodcols3")
    products(3 * UNROLL, slots, rows_s, row_split, False)
    phase("rowfar")
    opposite = xs[0] * 2 * count
    for d, (yy, peer) in enumerate([(1 - yhi, across), (yhi, (r, col_of(yhi, xs[0], core)))]):
        send(
            row_pair.at[:, pl.ds(pl.multiple_of(opposite + yy * count, count), count), :],
            row_far.at[d],
            ring_sem.at[2 + d],
            peer,
        )
    phase("scatcols")
    scatter(cols_v[...], part_cols)

    def lot(ref, k):
        return ref.at[:, pl.ds(pl.multiple_of(k * count, count), count), :]

    for d, zz in enumerate(zn):
        send(
            part_cols.at[:, pl.ds(pl.multiple_of(zz * 2 * count, 2 * count), 2 * count), :],
            col_near.at[d],
            back_sem.at[d],
            (row_of(zz, ylo), c),
        )
    send(lot(part_cols, far[0]), col_far.at[0], back_sem.at[2], far)
    phase("rownear")
    for d in range(2):
        arrived(row_near.at[d], ring_sem.at[d], (r, col_of(yhi, xn[1 - d], core)))
    mine_at = pl.multiple_of(x * 2 * count + yhi * count, count)
    away_at = pl.multiple_of(x * 2 * count + (1 - yhi) * count, count)
    for v in range(8):
        at = pl.ds(pl.multiple_of((1 - yhi) * count, count), count)
        row_send[v] = row_pair[v, pl.ds(away_at, count), :] + (row_near[0, v, at, :] + row_near[1, v, at, :])
    send(row_send, row_last, last_sem.at[0], (r, col_peer))
    phase("colfar")
    send(
        lot(part_cols, row_of(zs[0], ylo)), col_far.at[1], back_sem.at[3], (row_of(zs[0], ylo), c)
    )
    phase("near")
    for d in range(2):
        arrived(col_near.at[d], back_sem.at[d], (row_of(zn[1 - d], ylo), c))
    at = pl.multiple_of((1 - ylo) * count, count)
    away = lot(part_cols, row_peer)
    for v in range(8):
        col_send[v] = away[v] + (col_near[0, v, pl.ds(at, count), :] + col_near[1, v, pl.ds(at, count), :])
    send(col_send, col_last, last_sem.at[1], (row_peer, c))

    phase("waitfar")
    arrived(row_far.at[0], ring_sem.at[2], across)
    arrived(row_far.at[1], ring_sem.at[3], (r, col_of(yhi, xs[0], core)))
    arrived(col_far.at[0], back_sem.at[2], far)
    arrived(col_far.at[1], back_sem.at[3], (row_of(zs[0], ylo), c))
    home = pl.ds(pl.multiple_of(ylo * count, count), count)
    own = pl.ds(pl.multiple_of(yhi * count, count), count)
    col_mine = lot(part_cols, r)
    for v in range(8):
        total = (row_pair[v, pl.ds(mine_at, count), :] + col_mine[v]) + (col_far[0, v] + col_far[1, v])
        total = total + (row_far[0, v] + row_far[1, v])
        total = total + (row_near[0, v, own, :] + row_near[1, v, own, :])
        image[v * count : (v + 1) * count, :] = total + (col_near[0, v, home, :] + col_near[1, v, home, :])
    phase("early1")
    for peer in row_back:
        arrived(early_one.at[peer[1]], one_sem.at[peer[1]], peer)
    total = early_one[0]
    for i in range(1, early_one.shape[0]):
        total = total + early_one[i]
    early_send[1] = total
    early_two[r] = total
    for peer in col_group:
        send(early_send.at[1], early_two.at[r], two_sem.at[r], peer)
    phase("waitlast")
    arrived(col_last, last_sem.at[1], (row_peer, c))
    arrived(row_last, last_sem.at[0], (r, col_peer))
    phase("shifted")
    for v in range(8):
        part = slice(v * count, (v + 1) * count)
        image[part, :] = image[part, :] + (row_last[v] + col_last[v])
    for t in range(count):
        at = slice(t * 128, (t + 1) * 128)
        shifted[:, at] = image[pl.ds(t, 8, stride=count), :] + (diag[t : t + 1, :] - SHIFT) * now[:, at]

    phase("gram")
    halves = split_rows(shifted[...])
    gram = lax.dot_general(
        halves,
        jnp.concatenate([halves, known_split[0], known_split[1]], axis=0),
        NT_DIMS,
        preferred_element_type=F32,
    )
    gram = gram[0:8] + gram[8:16]
    place, lane = iota((48, 256), 0), iota((48, 256), 1)
    block = jnp.where(place < 16, 0, 1 + (place // 8) % 2)
    spread = ((lane // 64 == block) & (lane % 8 == place % 8)).astype(F32).astype(BF16)
    flat = lax.dot_general(three_parts(gram), spread, NN_DIMS, preferred_element_type=F32)
    flat = (flat[0:8] + flat[8:16]) + flat[16:24]
    flat = jnp.where((iota((8, 256), 1) // 8) % 8 == iota((8, 256), 0), flat, 0.0)
    flat = jnp.sum(flat, axis=0, keepdims=True)
    final_send[0:1, :] = flat[:, 0:128]
    final_send[1:2, :] = flat[:, 128:256]
    phase("final")
    me = r * early_one.shape[0] + c
    own_copy = pltpu.make_async_copy(final_send, final_all.at[me], in_sem.at[2])
    own_copy.start()
    steps = sorted(
        itertools.product(range(4), range(2), range(2), range(4), range(2)),
        key=lambda s: -(min(s[0], 4 - s[0]) + s[1] + 2 * s[2] + min(s[3], 4 - s[3])),
    )
    steps.remove((0, 0, 0, 0, 0))
    lasts = []
    for a, b, d, e, f in steps:
        peer = (
            row_of((z + a) % 4, (ylo + b) % 2),
            col_of((yhi + d) % 2, (x + e) % 4, (core + f) % 2),
        )
        copy = pltpu.make_async_remote_copy(
            src_ref=final_send,
            dst_ref=final_all.at[me],
            send_sem=all_sem.at[0],
            recv_sem=all_sem.at[1],
            device_id=peer,
            device_id_type=MESH,
        )
        copy.start()
        lasts.append(peer)
    phase("early2")
    for peer in col_back:
        arrived(early_two.at[peer[0]], two_sem.at[peer[0]], peer)
    total = early_two[0]
    for i in range(1, early_two.shape[0]):
        total = total + early_two[i]
    early_out[...] = total

    phase("waitfinal")
    own_copy.wait()
    others = final_all.at[0 : len(steps)]
    waiter = pltpu.make_async_remote_copy(
        src_ref=others,
        dst_ref=others,
        send_sem=all_sem.at[0],
        recv_sem=all_sem.at[1],
        device_id=lasts[0],
        device_id_type=MESH,
    )
    waiter.wait_recv()
    phase("sum")
    final_out[...] = jnp.sum(final_all[...], axis=0)
    phase("waitsends")
    for copy in sends:
        copy.wait_send()
    waiter.wait_send()
    phase(None)


def finish(scale, shifted, early, final, now, prev, coupling, next_out, alpha_out, beta_out):
    open_scope = []

    def phase(name):
        if open_scope:
            open_scope.pop().__exit__(None, None, None)
        if name:
            open_scope.append(jax.named_scope(name))
            open_scope[0].__enter__()

    phase("Bgram")
    line, lane = iota((8, 16), 0), iota((8, 16), 1)
    flat = jnp.concatenate([final[0:1, :], final[1:2, :]], axis=1) * scale
    flat = jnp.where((iota((8, 256), 1) // 8) % 8 == iota((8, 256), 0), flat, 0.0)
    parts = three_parts(flat)
    place, at = iota((16, 256), 0), iota((16, 256), 1)

    def gathered(block):
        pick = ((at // 64 == block) & (at % 8 == place % 8)).astype(F32).astype(BF16)
        out = lax.dot_general(parts, pick, NT_DIMS, preferred_element_type=F32)
        return (out[0:8] + out[8:16]) + out[16:24]

    cross = gathered(1 + place // 8)
    square = gathered(jnp.where(place < 8, 0, -1))
    known = early[:, 0:16] * scale
    eye = (line == lane).astype(F32)
    shift_eye = (line + 8 == lane).astype(F32)
    coupled = dot_exact(coupling[...], shift_eye, NN_DIMS)
    alpha_t = cross + SHIFT * known[0:8]
    weights = jnp.where(lane < 8, SHIFT * eye - alpha_t, -coupled)
    zeros = jnp.zeros((8, 16), F32)
    mixed = cross + 0.5 * dot_exact(weights, known, NN_DIMS)
    once = dot_exact(mixed, jnp.concatenate([weights, zeros], axis=0), NT_DIMS)
    again = dot_exact(weights, jnp.concatenate([mixed, zeros], axis=0), NT_DIMS)
    residual = shifted[...] + dot_exact(
        weights, jnp.concatenate([now[...], prev[...]], axis=0), NN_DIMS
    )
    phase("Bchol")
    gram = square + (once + again)

    def entry(a, b):
        return jnp.broadcast_to(gram[a : a + 1, b : b + 1], (8, 128))

    upper = {(a, b): entry(a, b) for a in range(8) for b in range(a, 8)}
    inverse = {}
    for a in range(8):
        pivot = 1.0 / upper[a, a]
        for b in range(a + 1, 8):
            factor = upper[a, b] * pivot
            for k in range(b, 8):
                upper[b, k] = upper[b, k] - factor * upper[a, k]
            for k in range(a):
                inverse[b, k] = inverse[b, k] - factor * inverse[a, k]
            inverse[b, a] = -factor
    line, lane = iota((8, 128), 0), iota((8, 128), 1)
    solve = jnp.zeros((8, 128), F32)
    beta = jnp.zeros((8, 128), F32)
    for a in range(8):
        root = jnp.sqrt(upper[a, a])
        scale_row = 1.0 / root
        solve = jnp.where((line == a) & (lane == a), scale_row, solve)
        beta = jnp.where((line == a) & (lane == a), root, beta)
        for k in range(a):
            solve = jnp.where((line == a) & (lane == k), inverse[a, k] * scale_row, solve)
        for b in range(a + 1, 8):
            beta = jnp.where((line == a) & (lane == b), upper[a, b] * scale_row, beta)
    phase("Bsolve")
    next_out[...] = dot_exact(solve[:, 0:8], residual, NN_DIMS)
    beta_out[...] = beta[:, 0:8]
    alpha_out[...] = dot_exact(eye[:, 0:8], alpha_t[:, 0:8], NT_DIMS)
    phase(None)


def local(tiles, tile_rows, tile_cols, tile_counts, block_now, block_prev, coupling, diag_energy):
    slots, tile_width = tiles.shape[2], tiles.shape[3]
    vectors, width = block_now.shape
    n_row, n_col = lax.axis_size("row"), lax.axis_size("col")
    count = width // tile_width
    rows, cols = tile_rows.reshape(1, slots), tile_cols.reshape(1, slots)
    hbm = pl.BlockSpec(memory_space=pltpu.HBM)
    vmem = pl.BlockSpec(memory_space=pltpu.VMEM)
    dma = pltpu.SemaphoreType.DMA
    n_rt, n_ct = n_col * count, n_row * count
    shape = jax.ShapeDtypeStruct
    shifted, early, final = pl.pallas_call(
        kernel,
        out_shape=(shape((vectors, width), F32), shape((16, 128), F32), shape((2, 128), F32)),
        in_specs=[hbm] * 9,
        out_specs=(vmem, vmem, vmem),
        scratch_shapes=[
            pltpu.VMEM((slots, tile_width, tile_width), F32),
            pltpu.VMEM((slots, tile_width, tile_width), BF16),
            pltpu.VMEM((slots, tile_width, tile_width), BF16),
            pltpu.SMEM((slots,), jnp.int32),
            pltpu.SMEM((slots,), jnp.int32),
            pltpu.SMEM((1, 1), jnp.int32),
            pltpu.VMEM((1, slots), jnp.int32),
            pltpu.VMEM((1, slots), jnp.int32),
            pltpu.VMEM((2 * vectors, width), F32),
            pltpu.VMEM((count, tile_width), F32),
            pltpu.VMEM((vectors, n_row * width), F32),
            pltpu.VMEM((vectors, n_col * width), F32),
            pltpu.VMEM((n_ct, 16, tile_width), BF16),
            pltpu.VMEM((n_rt, 16, tile_width), BF16),
            pltpu.VMEM((vectors * slots, tile_width), F32),
            pltpu.VMEM((vectors, n_rt, tile_width), F32),
            pltpu.VMEM((vectors, n_ct, tile_width), F32),
            pltpu.VMEM((vectors, n_rt // 2, tile_width), F32),
            pltpu.VMEM((2, vectors, 2 * count, tile_width), F32),
            pltpu.VMEM((2, vectors, count, tile_width), F32),
            pltpu.VMEM((vectors, count, tile_width), F32),
            pltpu.VMEM((vectors, count, tile_width), F32),
            pltpu.VMEM((2, vectors, 2 * count, tile_width), F32),
            pltpu.VMEM((2, vectors, count, tile_width), F32),
            pltpu.VMEM((vectors, count, tile_width), F32),
            pltpu.VMEM((vectors, count, tile_width), F32),
            pltpu.VMEM((vectors * count, tile_width), F32),
            pltpu.VMEM((2, 16, 128), F32),
            pltpu.VMEM((n_col, 16, 128), F32),
            pltpu.VMEM((n_row, 16, 128), F32),
            pltpu.VMEM((2, 128), F32),
            pltpu.VMEM((n_row * n_col, 2, 128), F32),
            pltpu.VMEM((2, 16, width), BF16),
            dma((slots // CHUNK,)),
            dma((8,)),
            dma((64,)),
            dma((n_row,)),
            dma((n_col,)),
            dma((1,)),
            dma((4,)),
            dma((2,)),
            dma((4,)),
            dma((n_col,)),
            dma((n_row,)),
            dma((2,)),
        ],
        compiler_params=pltpu.CompilerParams(
            collective_id=0, has_side_effects=True, vmem_limit_bytes=52 * 2**20
        ),
    )(
        *(
            value if value is tile_counts else pltpu.with_memory_space_constraint(value, pltpu.HBM)
            for value in (
                tiles.reshape(slots, tile_width, tile_width),
                rows.reshape(slots),
                cols.reshape(slots),
                tile_counts,
                rows,
                cols,
                block_now,
                block_prev,
                diag_energy.reshape(count, tile_width),
            )
        )
    )
    return pl.pallas_call(
        functools.partial(finish, 1.0 / (width * n_row * n_col)),
        out_shape=(shape((vectors, width), F32), shape((8, 8), F32), shape((8, 8), F32)),
        in_specs=[vmem] * 6,
        out_specs=(vmem, vmem, vmem),
        compiler_params=pltpu.CompilerParams(vmem_limit_bytes=4 * 2**20),
    )(shifted, early, final, block_now, block_prev, coupling)


def solution(mesh):
    return jax.shard_map(
        local,
        mesh=mesh,
        in_specs=(
            P("row", "col", None, None, None),
            P("row", "col", None),
            P("row", "col", None),
            P("row", "col"),
            P(None, ("row", "col")),
            P(None, ("row", "col")),
            P(),
            P(("row", "col")),
        ),
        out_specs=(P(None, ("row", "col")), P(), P()),
        check_vma=False,
    )
```
